32 devices in a mesh: ctx: 16 (over z, x, core), head: 2 (over y).
Axes of the slice: x: 2, y: 2, z: 4, core: 2. Of those that a mesh axis runs over, the one named last changes fastest.
Arguments:
- queries: bfloat16 [2048, 64, 576], P('ctx', 'head'), may hold values from -512 to 512
- latents: bfloat16 [2048, 576], P('ctx'), may hold values from -4 to 4
- index_queries: bfloat16 [2048, 64, 128], P('ctx', 'head'), may hold values from -512 to 512
- index_keys: bfloat16 [2048, 128], P('ctx'), may hold values from -4 to 4
- head_weights: float32 [2048, 64], P('ctx', 'head'), may hold values from -1.5 to 1.5
- block_pos: int32 [16], replicated, may hold values from 0 to 15, each once
Outputs:
- grad_index_queries: float32 [2048, 64, 128], P('ctx', 'head')
- grad_index_keys: float32 [2048, 128], P('ctx')
The draws below stay inside these ranges and needn't reach their ends.
All inputs are finite; a program needn't handle non-finite values.
Results may differ from the reference program's by a relative error of at most 0.008.
Values may be sent and summed in bfloat16 or wider, within the bound.
A program may use at most 128 MiB of HBM per device.

```python
import jax
import jax.numpy as jnp
from jax import lax

HEADS = 64
RANK = 576
IHEADS = 64
IDIM = 128
TOK_DEV = 128
SEQ = 2048
BLOCKS = 16


def context_draw(key):
    pieces = jax.random.split(jax.random.fold_in(key, 7), 5)
    latent = jnp.clip(jax.random.normal(pieces[0], (SEQ, RANK), jnp.float32), -4.0, 4.0)
    latent = latent.astype(jnp.bfloat16).astype(jnp.float32)
    ikeys = jnp.clip(jax.random.normal(pieces[1], (SEQ, IDIM), jnp.float32), -4.0, 4.0)
    ikeys = ikeys.astype(jnp.bfloat16).astype(jnp.float32)
    weights = jnp.clip(0.3 * jax.random.normal(pieces[2], (SEQ, IHEADS), jnp.float32), -1.5, 1.5)
    query = jnp.clip(jax.random.normal(pieces[3], (SEQ, HEADS, RANK), jnp.float32), -4.0, 4.0)
    iquery = jnp.clip(jax.random.normal(pieces[4], (SEQ, IHEADS, IDIM), jnp.float32), -4.0, 4.0)
    return (latent, ikeys, weights, query, iquery)


def draw_latents(key, part):
    return context_draw(key)[0].astype(jnp.bfloat16)


def draw_index_keys(key, part):
    return context_draw(key)[1].astype(jnp.bfloat16)


def draw_head_weights(key, part):
    return context_draw(key)[2]


def draw_queries(key, part):
    return context_draw(key)[3].astype(jnp.bfloat16)


def draw_index_queries(key, part):
    return context_draw(key)[4].astype(jnp.bfloat16)


def setup_inputs(seed: int = 0) -> dict:
    seeds = jax.random.split(jax.random.key(seed), 7)
    return {
        "queries": draw_queries(jax.random.fold_in(seeds[6], 71), 0),
        "latents": draw_latents(jax.random.fold_in(seeds[6], 71), 0),
        "index_queries": draw_index_queries(jax.random.fold_in(seeds[6], 71), 0),
        "index_keys": draw_index_keys(jax.random.fold_in(seeds[6], 71), 0),
        "head_weights": draw_head_weights(jax.random.fold_in(seeds[6], 71), 0),
        "block_pos": jax.random.permutation(seeds[5], BLOCKS).astype(jnp.int32),
    }


SCALE_ATTN = 192.0 ** -0.5
LOSS_SCALE = 1024.0
NEGATIVE = -1.0e30


def positions(block_pos):
    stored = jnp.arange(SEQ, dtype=jnp.int32)
    return block_pos[stored // TOK_DEV] * TOK_DEV + stored % TOK_DEV


def reference(queries, latents, index_queries, index_keys, head_weights, block_pos):
    place = positions(block_pos)
    visible = place[None, :] <= place[:, None]
    index_scale = IDIM ** -0.5
    latent_wide = latents.astype(jnp.float32)
    keys_wide = index_keys.astype(jnp.float32)

    def attend(summed, query_head):
        scores = SCALE_ATTN * jnp.dot(query_head.astype(jnp.float32), latent_wide.T, precision=lax.Precision.HIGHEST)
        scores = jnp.where(visible, scores, NEGATIVE)
        row_top = jnp.max(scores, axis=1, keepdims=True)
        weights = jnp.where(visible, jnp.exp(scores - row_top), 0.0)
        return summed + weights / jnp.sum(weights, axis=1, keepdims=True), None

    target, _ = lax.scan(attend, jnp.zeros((SEQ, SEQ), jnp.float32), jnp.swapaxes(queries, 0, 1))
    target = target / HEADS

    def index_head(summed, inputs):
        query_head, weight = inputs
        dots = jnp.dot(query_head.astype(jnp.float32), keys_wide.T, precision=lax.Precision.HIGHEST)
        return summed + weight[:, None] * jnp.maximum(dots, 0.0) * index_scale, None

    stacked = (jnp.swapaxes(index_queries, 0, 1), head_weights.T)
    index, _ = lax.scan(index_head, jnp.zeros((SEQ, SEQ), jnp.float32), stacked)
    masked = jnp.where(visible, index, NEGATIVE)
    row_top = jnp.max(masked, axis=1, keepdims=True)
    weights = jnp.where(visible, jnp.exp(masked - row_top), 0.0)
    prob = weights / jnp.sum(weights, axis=1, keepdims=True)
    delta = jnp.where(visible, LOSS_SCALE * (prob - target), 0.0).astype(jnp.bfloat16)
    delta_wide = lax.optimization_barrier(delta).astype(jnp.float32)

    def backward(summed, inputs):
        query_head, weight = inputs
        query_wide = query_head.astype(jnp.float32)
        dots = jnp.dot(query_wide, keys_wide.T, precision=lax.Precision.HIGHEST)
        coef = jnp.where(dots > 0.0, delta_wide * weight[:, None] * index_scale, 0.0).astype(jnp.bfloat16)
        coef = lax.optimization_barrier(coef).astype(jnp.float32)
        grad_query = jnp.dot(coef, keys_wide, precision=lax.Precision.HIGHEST)
        return summed + jnp.dot(coef.T, query_wide, precision=lax.Precision.HIGHEST), grad_query

    grad_keys, grad_queries = lax.scan(backward, jnp.zeros((SEQ, IDIM), jnp.float32), stacked)
    return jnp.swapaxes(grad_queries, 0, 1), grad_keys
```

```python
import functools
import math

import jax
import jax.numpy as jnp
from jax import lax
from jax.experimental import pallas as pl
from jax.experimental.pallas import tpu as pltpu
from jax.sharding import PartitionSpec as P

HEADS = 64
SCALE_ATTN = 192.0 ** (-0.5)
LOSS_SCALE = 1024.0
NEGATIVE = -1e30
LOG2E = math.log2(math.e)
MESH = pl.DeviceIdType.MESH
F32 = jnp.float32
BF16 = jnp.bfloat16
TOK = 8
ITOK = 8
PIECES = 2
RUN = 64
GROUP = 8
WEIGHTS = (1, 3, 4)
VMEM_LIMIT = 60 * 1024 * 1024


def place(n):
    me = lax.axis_index("ctx")
    a = n // 4
    return me // 4, (me // 2) % 2, me % 2, a


def at(z, x, c):
    return (z * 2 + x) * 2 + c


def remote(src, dst, send, recv, **where):
    return pltpu.make_async_remote_copy(
        src_ref=src, dst_ref=dst, send_sem=send, recv_sem=recv, device_id=where, device_id_type=MESH
    )


def dot_t(a, b):
    return lax.dot_general(a, b, (((1,), (1,)), ((), ())), preferred_element_type=F32)


def gather_kernel(
    n, heads, lat_ref, key_ref, iq_ref, w_ref, lat_out, key_out, idx_ref,
    scr_a, scr_b, send_sem, recv_sem, own_sem,
):
    z, x, c, a = place(n)
    y = lax.axis_index("head")
    other_y = y + 1 - 2 * (y % 2)
    partner = at(z, x, 1 - c)
    barrier = pltpu.get_barrier_semaphore()

    def greet(**where):
        pl.semaphore_signal(barrier, inc=1, device_id=where, device_id_type=MESH)

    greet(ctx=at(z, 1 - x, c))
    greet(ctx=partner)
    greet(head=other_y)

    for d in range(1, a):
        greet(ctx=at((z + d) % a, x, c))

    me = at(z, x, c)
    owns = []
    for k, (src, dst) in enumerate(((key_ref, key_out), (lat_ref, lat_out))):
        own = pltpu.make_async_copy(src, dst.at[me], own_sem.at[k])
        own.start()
        owns.append(own)
    pl.semaphore_wait(barrier, 2 + a)

    rows = lat_ref.shape[0]
    part = rows // 2

    def piece(ref, k):
        return ref.at[pl.ds(pl.multiple_of((k - 1) * part, part), part)]

    def copy(k, slot, way, first, **where):
        if isinstance(k, int) and k == 0:
            src, dst = (key_ref if first else key_out.at[slot]), key_out.at[slot]
        else:
            dst = piece(lat_out.at[slot], k)
            src = piece(lat_ref, k) if first else dst
        return remote(src, dst, send_sem.at[k, slot, way], recv_sem.at[k, slot], **where)

    def to_core(k, slot, first=False):
        return copy(k, slot, 0, first, ctx=partner)

    def to_x(k, slot, first=False):
        return copy(k, slot, 1, first, ctx=at(z, 1 - x, c))

    def to_y(k, slot):
        return copy(k, slot, 2, False, head=other_y)

    def arrived(k, slot):
        to_core(k, slot).wait_recv()

    def line(k, slot, act):
        for d in range(1, a):
            act(copy(k, slot, 4 + d, True, ctx=at((z + d) % a, x, c)))

    def sides(d, act):
        for side in (1, -1) if d > 0 else (0,):
            zs = z - d if side >= 0 else z + d
            if d == 0:
                act(zs, side)
            else:
                ok = zs >= 0 if side > 0 else zs < a
                pl.when(ok)(functools.partial(act, zs, side))

    start = lambda item: item.start()
    done = lambda item: item.wait_send()
    mine, others = 1 + y % 2, 2 - y % 2

    def column(ks, d, wait, act):
        def go(zs, side):
            slot = at(zs, x, c)
            for k in ks:
                if wait and d > 0:
                    arrived(k, slot)
                if d == 0:
                    line(k, slot, act)
            crossing = 0 if ks == (0,) else mine
            act(to_x(crossing, slot, d == 0))
            for k in ks:
                act(to_core(k, slot, d == 0))

        sides(d, go)

    def crossed(k, d, wait, act, onward):
        def go(zs, side):
            slot = at(zs, 1 - x, c)
            if wait:
                arrived(k, slot)
            if onward:
                act(to_y(k, slot))
            act(to_core(k, slot))

        sides(d, go)

    column((0,), 0, True, start)
    for d in range(1, a):
        column((0,), d, True, start)
    column((1, 2), 0, True, start)
    for d in range(a):
        crossed(0, d, True, start, False)

    owns[0].wait()
    for zs in range(a):
        for xs in range(2):
            arrived(0, at(zs, xs, 1 - c))

    stages = []
    for d in range(a + 2):
        if 1 <= d < a:
            stages.append(functools.partial(column, (1, 2), d, True, start))
        if 1 <= d <= a:
            stages.append(functools.partial(crossed, mine, d - 1, True, start, True))
        if 2 <= d:
            stages.append(functools.partial(crossed, others, d - 2, True, start, False))

    depth = iq_ref.shape[1]
    m = ITOK * heads
    width = 4 * rows

    def index_chunk(i, _):
        iq = iq_ref[pl.ds(pl.multiple_of(i * m, m), m), :]
        w = w_ref.at[pl.ds(pl.multiple_of(i * m, m), m)]
        out = idx_ref.at[pl.ds(pl.multiple_of(i * ITOK, ITOK), ITOK)]
        scrs = (scr_a, scr_b)

        def reduce(p):
            scr = scrs[p % 2]
            sums = []
            for t in range(ITOK):
                acc = None
                for g in range(0, heads, 8):
                    r = t * heads + g
                    term = jnp.maximum(scr[r : r + 8, :], 0.0) * jnp.concatenate(
                        [w[r : r + 8, :]] * (width // 128), axis=1
                    )
                    acc = term if acc is None else acc + term
                sums.append(jnp.sum(acc, axis=0, keepdims=True))
            out[:, p * width : (p + 1) * width] = jnp.concatenate(sums, axis=0)

        count = n * rows // width
        per = width // rows
        for p in range(count):
            held = key_out[p * per : (p + 1) * per].reshape(width, depth)
            scrs[p % 2][...] = dot_t(iq, held)
            if p > 0:
                reduce(p - 1)
        reduce(count - 1)
        return 0

    chunks = iq_ref.shape[0] // m
    lead = chunks // 4
    count = len(stages)
    cut = [0] + [lead + (chunks - lead) * d // count for d in range(count)] + [chunks]
    for d in range(count + 1):
        if cut[d + 1] > cut[d]:
            lax.fori_loop(cut[d], cut[d + 1], index_chunk, 0)
        if d < count:
            stages[d]()

    owns[1].wait()
    for zs in range(a):
        for xs in range(2):
            for k in (1, 2):
                arrived(k, at(zs, xs, 1 - c))
    for ks in ((0,), (1, 2)):
        for d in range(a):
            column(ks, d, False, done)
    for d in range(a):
        crossed(0, d, False, done, False)
        crossed(mine, d, False, done, True)
        crossed(others, d, False, done, False)


def gather(latents, keys, iq, wide, heads, n):
    rows = latents.shape[0]
    seq = rows * n
    hbm = pl.BlockSpec(memory_space=pl.ANY)
    vmem = pl.BlockSpec(memory_space=pltpu.VMEM)
    m = ITOK * heads
    return pl.pallas_call(
        functools.partial(gather_kernel, n, heads),
        out_shape=(
            jax.ShapeDtypeStruct((n, rows, latents.shape[1]), BF16),
            jax.ShapeDtypeStruct((n, rows, keys.shape[1]), BF16),
            jax.ShapeDtypeStruct((iq.shape[0] // heads, seq), F32),
        ),
        in_specs=[hbm, hbm, vmem, vmem],
        out_specs=(hbm, vmem, vmem),
        scratch_shapes=[
            pltpu.VMEM((m, 4 * rows), F32),
            pltpu.VMEM((m, 4 * rows), F32),
            pltpu.SemaphoreType.DMA((3, n, 4 + n // 4)),
            pltpu.SemaphoreType.DMA((3, n)),
            pltpu.SemaphoreType.DMA((2,)),
        ],
        compiler_params=pltpu.CompilerParams(
            collective_id=0, has_side_effects=True, vmem_limit_bytes=VMEM_LIMIT
        ),
        name="gather",
    )(latents, keys, iq, wide)


def attend_kernel(
    half, n, q_ref, lat_ref, pos_ref, mine_ref, out_ref, low_ref, scr_a, scr_b, top_a, top_b, wide, acc
):
    step = pl.program_id(0)
    seq, depth = lat_ref.shape
    group, _, lanes = q_ref.shape
    count = lanes // 2
    rows = seq // n
    edge = depth // 128 * 128

    @pl.when(step == 0)
    def _():
        lane = lax.broadcasted_iota(jnp.int32, (rows, lanes), 1)
        row = lax.broadcasted_iota(jnp.int32, (rows, lanes), 0)
        own = jnp.where(row <= half * count + lane - (lanes - count), 0.0, NEGATIVE)
        for b in range(n):
            ahead = pos_ref[b] - mine_ref[0]
            bias = jnp.where(ahead == 0, own, jnp.where(ahead < 0, 0.0, NEGATIVE))
            at = slice(b * rows, (b + 1) * rows)
            wide[at, :edge] = lat_ref[at, :edge]
            last = lat_ref[at, edge:].astype(F32)
            last = jnp.concatenate([last, jnp.zeros((rows, lanes - last.shape[1]), F32)], axis=1)
            wide[at, edge:] = jnp.where(lane < depth - edge, last, bias).astype(BF16)
        scr_b[...] = jnp.zeros_like(scr_b)
        top_b[...] = jnp.zeros_like(top_b)
        acc[...] = jnp.zeros_like(acc)

    def scores(first, scr, top_ref):
        def part(h):
            return q_ref[h][:, half * count : (half + 1) * count]

        weights = jnp.concatenate([part(first + h) for h in range(4)], axis=1)
        line = lax.broadcasted_iota(jnp.int32, (count, 4 * count), 0)
        column = lax.broadcasted_iota(jnp.int32, (count, 4 * count), 1)
        same = jnp.where(lax.rem(column, count) == line, 1.0, 0.0).astype(BF16)
        weights = jnp.concatenate([weights, same], axis=0)
        piece = seq // PIECES
        top = None
        for r in range(0, seq, piece):
            v = jnp.dot(wide[r : r + piece, :], weights, preferred_element_type=F32)
            scr[r : r + piece, :] = v
            for k in range(0, piece, 8):
                top = v[k : k + 8] if top is None else jnp.maximum(top, v[k : k + 8])
            yield
        top_ref[...] = top

    def softmax(scr, top_ref, use):
        scale = []
        for tile in (slice(0, lanes), slice(lanes, 2 * lanes)):
            top = jnp.max(top_ref[:, tile], axis=0, keepdims=True)
            total = None
            for r in range(0, seq, RUN):
                p = jnp.exp2((scr[r : r + RUN, tile] - top) * (SCALE_ATTN * LOG2E))
                scr[r : r + RUN, tile] = p
                total = p if total is None else total + p
                yield
            total = jnp.sum(total, axis=0, keepdims=True)
            share = 1.0 / (HEADS * total)
            scale.append(share if use is None else jnp.where(use, share, 0.0))
        for r in range(0, seq, RUN):
            acc[r : r + RUN, :] += (
                scr[r : r + RUN, :lanes] * scale[0] + scr[r : r + RUN, lanes:] * scale[1]
            )
            yield

    def together(dots, vectors):
        total = 3 * (seq // RUN)
        done = 0
        for k, _ in enumerate(dots):
            upto = -(-total * WEIGHTS[k] // WEIGHTS[-1])
            while done < upto:
                next(vectors, None)
                done += 1
        for _ in vectors:
            pass

    for k in range(0, group, 8):
        together(scores(k, scr_a, top_a), softmax(scr_b, top_b, step > 0 if k == 0 else None))
        together(scores(k + 4, scr_b, top_b), softmax(scr_a, top_a, None))

    @pl.when(step == pl.num_programs(0) - 1)
    def _():
        for _ in softmax(scr_b, top_b, None):
            pass
        both = jnp.transpose(acc[...])
        out = both[:count] + both[count:]
        out_ref[...] = out
        low_ref[...] = out.astype(BF16)


def attend(q, lat, block_pos, mine, half, n):
    heads, depth, lanes = q.shape
    seq = lat.shape[0]
    count = lanes // 2
    smem = pl.BlockSpec(memory_space=pltpu.SMEM)
    whole = lambda i: (0, 0)
    return pl.pallas_call(
        functools.partial(attend_kernel, half, n),
        grid=(heads // GROUP,),
        out_shape=(
            jax.ShapeDtypeStruct((count, seq), F32),
            jax.ShapeDtypeStruct((count, seq), BF16),
        ),
        in_specs=[
            pl.BlockSpec((GROUP, depth, lanes), lambda i: (i, 0, 0)),
            pl.BlockSpec((seq, depth), whole),
            smem,
            smem,
        ],
        out_specs=(pl.BlockSpec((count, seq), whole), pl.BlockSpec((count, seq), whole)),
        scratch_shapes=[
            pltpu.VMEM((seq, 2 * lanes), F32),
            pltpu.VMEM((seq, 2 * lanes), F32),
            pltpu.VMEM((8, 2 * lanes), F32),
            pltpu.VMEM((8, 2 * lanes), F32),
            pltpu.VMEM((seq, depth + count), BF16),
            pltpu.VMEM((seq, lanes), F32),
        ],
        compiler_params=pltpu.CompilerParams(vmem_limit_bytes=VMEM_LIMIT),
        cost_estimate=pl.CostEstimate(
            flops=count * heads * seq * depth // 8,
            bytes_accessed=4 * count * heads * depth,
            transcendentals=0,
        ),
        name="attend",
    )(q, lat, block_pos, mine)


def back_kernel(heads, last, iq_ref, w_ref, key_ref, post_ref, poss_ref, *rest):
    peers_i = rest[0]
    own_i, own_t, peers_t = rest[1:4]
    gq_ref, gk_ref, scr, coef, acc, dscr = rest[-6:]
    step = pl.program_id(0)

    @pl.when(step == 0)
    def _():
        acc[...] = rest[4][...] if last else jnp.zeros_like(acc)

    scr[...] = dot_t(iq_ref[...], key_ref[...])
    index, target = own_i[...], own_t[...]
    for k in range(peers_i.shape[0]):
        index = index + peers_i[k]
        target = target + peers_t[k].astype(F32)
    seen = poss_ref[...] <= post_ref[...]
    masked = jnp.where(seen, index, NEGATIVE)
    weights = jnp.where(seen, jnp.exp(masked - jnp.max(masked, axis=1, keepdims=True)), 0.0)
    prob = weights * (1.0 / jnp.sum(weights, axis=1, keepdims=True))
    dscr[...] = jnp.where(seen, LOSS_SCALE * (prob - target), 0.0).astype(BF16).astype(F32)
    for t in range(TOK):
        for g in range(0, heads, 8):
            r = t * heads + g
            wide = jnp.concatenate([w_ref[r : r + 8, :]] * (dscr.shape[1] // 128), axis=1)
            value = dscr[t : t + 1, :] * wide
            coef[r : r + 8, :] = jnp.where(scr[r : r + 8, :] > 0.0, value, 0.0).astype(BF16)
    gq_ref[...] = jnp.dot(coef[...], key_ref[...], preferred_element_type=F32)
    acc[...] += lax.dot_general(
        iq_ref[...], coef[...], (((0,), (0,)), ((), ())), preferred_element_type=F32
    )

    @pl.when(step == pl.num_programs(0) - 1)
    def _():
        if last:
            gk_ref[...] = jnp.transpose(acc[...]).astype(BF16)
        else:
            gk_ref[...] = acc[...]


def back(iq, wide, keys, pos_t, pos_s, peers_i, own_i, own_t, peers_t, carried, heads, first, last):
    depth = iq.shape[1]
    seq = keys.shape[0]
    count = own_t.shape[0]
    m = TOK * heads
    off = first // TOK
    others = peers_i.shape[0]
    return pl.pallas_call(
        functools.partial(back_kernel, heads, last),
        grid=(count // TOK,),
        out_shape=(
            jax.ShapeDtypeStruct(iq.shape, F32),
            jax.ShapeDtypeStruct((seq, depth), BF16)
            if last
            else jax.ShapeDtypeStruct((depth, seq), F32),
        ),
        in_specs=[
            pl.BlockSpec((m, depth), lambda i: (i + off, 0)),
            pl.BlockSpec((m, wide.shape[1]), lambda i: (i + off, 0)),
            pl.BlockSpec((seq, depth), lambda i: (0, 0)),
            pl.BlockSpec((TOK, 1), lambda i: (i + off, 0)),
            pl.BlockSpec((1, seq), lambda i: (0, 0)),
            pl.BlockSpec((others, TOK, seq), lambda i: (0, i + off, 0)),
            pl.BlockSpec((TOK, seq), lambda i: (i + off, 0)),
            pl.BlockSpec((TOK, seq), lambda i: (i, 0)),
            pl.BlockSpec((others, TOK, seq), lambda i: (0, i, 0)),
        ]
        + [pl.BlockSpec((depth, seq), lambda i: (0, 0)), pl.BlockSpec(memory_space=pl.ANY)] * last,
        input_output_aliases={10: 0} if last else {},
        out_specs=(
            pl.BlockSpec((m, depth), lambda i: (i + off, 0)),
            pl.BlockSpec((seq, depth) if last else (depth, seq), lambda i: (0, 0)),
        ),
        scratch_shapes=[
            pltpu.VMEM((m, seq), F32),
            pltpu.VMEM((m, seq), BF16),
            pltpu.VMEM((depth, seq), F32),
            pltpu.VMEM((TOK, seq), F32),
        ],
        compiler_params=pltpu.CompilerParams(vmem_limit_bytes=VMEM_LIMIT),
        cost_estimate=pl.CostEstimate(
            flops=8 * count * heads * seq * depth,
            bytes_accessed=8 * count * heads * depth,
            transcendentals=0,
        ),
        name="back",
    )(iq, wide, keys, pos_t, pos_s, peers_i, own_i, own_t, peers_t, *carried)


def scatter_kernel(
    n, ranks, gk_ref, out_ref, got1, sum1, put2, got2, sum2, put3, got3, put4, got4, ssem, rsem
):
    z, x, c, a = place(n)
    y = lax.axis_index("head")
    barrier = pltpu.get_barrier_semaphore()
    greeted = [dict(ctx=at(z, 1 - x, c)), dict(ctx=at(z, x, 1 - c))]
    greeted += [dict(ctx=at(lax.rem(z + d, a), x, c)) for d in range(1, a)]
    greeted += [dict(head=lax.rem(y + d, ranks)) for d in range(1, ranks)]
    for where in greeted:
        pl.semaphore_signal(barrier, inc=1, device_id=where, device_id_type=MESH)
    pl.semaphore_wait(barrier, len(greeted))

    first = remote(gk_ref.at[:, :, 1 - c], got1, ssem.at[0], rsem.at[0], ctx=at(z, x, 1 - c))
    first.start()
    first.wait()
    sum1[...] = gk_ref[:, :, c].astype(F32) + got1[...].astype(F32)
    put2[...] = sum1[:, 1 - x].astype(BF16)
    second = remote(put2, got2, ssem.at[1], rsem.at[1], ctx=at(z, 1 - x, c))
    second.start()
    second.wait()
    sum2[...] = sum1[:, x] + got2[...].astype(F32)
    put3[...] = sum2[...].astype(BF16)
    third = []
    for d in range(1, a):
        to = lax.rem(z + d, a)
        item = remote(
            put3.at[to], got3.at[d - 1], ssem.at[1 + d], rsem.at[1 + d], ctx=at(to, x, c)
        )
        item.start()
        third.append(item)
    for item in third:
        item.wait()
    part = sum2[z]
    for d in range(1, a):
        part = part + got3[d - 1].astype(F32)
    put4[...] = part
    fourth = []
    for d in range(1, ranks):
        item = remote(
            put4,
            got4.at[d - 1],
            ssem.at[a + d],
            rsem.at[a + d],
            head=lax.rem(y + d, ranks),
        )
        item.start()
        fourth.append(item)
    for item in fourth:
        item.wait()
    part = put4[...]
    for d in range(1, ranks):
        part = part + got4[d - 1]
    out_ref[...] = part


def scatter(gk, n, ranks):
    a = n // 4
    rows, depth = gk.shape[0] // n, gk.shape[1]
    vmem = pl.BlockSpec(memory_space=pltpu.VMEM)
    return pl.pallas_call(
        functools.partial(scatter_kernel, n, ranks),
        out_shape=jax.ShapeDtypeStruct((rows, depth), F32),
        in_specs=[vmem],
        out_specs=vmem,
        scratch_shapes=[
            pltpu.VMEM((a, 2, rows, depth), BF16),
            pltpu.VMEM((a, 2, rows, depth), F32),
            pltpu.VMEM((a, rows, depth), BF16),
            pltpu.VMEM((a, rows, depth), BF16),
            pltpu.VMEM((a, rows, depth), F32),
            pltpu.VMEM((a, rows, depth), BF16),
            pltpu.VMEM((a - 1, rows, depth), BF16),
            pltpu.VMEM((rows, depth), F32),
            pltpu.VMEM((ranks - 1, rows, depth), F32),
            pltpu.SemaphoreType.DMA((a + ranks,)),
            pltpu.SemaphoreType.DMA((a + ranks,)),
        ],
        compiler_params=pltpu.CompilerParams(collective_id=1, has_side_effects=True),
        name="scatter",
    )(gk.reshape(a, 2, 2, rows, depth))


def swap(value, ranks):
    return jnp.stack(
        [
            lax.ppermute(value, "head", [(i, (i + d) % ranks) for i in range(ranks)])
            for d in range(1, ranks)
        ]
    )


def body(queries, latents, index_queries, index_keys, head_weights, block_pos):
    rows, heads, rank = queries.shape
    depth = index_queries.shape[2]
    n, ranks = lax.axis_size("ctx"), lax.axis_size("head")
    seq = rows * n
    q = jnp.transpose(queries, (1, 2, 0))
    iq = index_queries.reshape(rows * heads, depth)
    wide = jnp.broadcast_to(
        (head_weights * depth ** (-0.5))[:, :, None], (rows, heads, 128)
    ).reshape(rows * heads, 128)
    local = jnp.arange(rows, dtype=jnp.int32)
    pos_s = (block_pos[:, None] * rows + local[None, :]).reshape(1, seq)
    mine = jnp.sum(jnp.where(jnp.arange(n) == lax.axis_index("ctx"), block_pos, 0))
    pos_t = (mine * rows + local)[:, None]

    lat, keys, own_i = gather(latents, index_keys, iq, wide, heads, n)
    lat = lat.reshape(seq, rank)
    keys = keys.reshape(seq, depth)
    peers_i = swap(own_i, ranks)
    own_t, peers_t = [], []
    for k in range(2):
        full, low = attend(q, lat, block_pos, mine[None], k, n)
        own_t.append(full)
        peers_t.append(swap(low, ranks))
    grads = ()
    for k in range(2):
        grad_queries, carry = back(
            iq, wide, keys, pos_t, pos_s, peers_i, own_i, own_t[k], peers_t[k], grads, heads,
            k * (rows // 2), k == 1,
        )
        grads = (carry, grad_queries)
    return grad_queries.reshape(rows, heads, depth), scatter(carry, n, ranks)


def solution(mesh):
    return jax.shard_map(
        body,
        mesh=mesh,
        in_specs=(
            P("ctx", "head", None),
            P("ctx", None),
            P("ctx", "head", None),
            P("ctx", None),
            P("ctx", "head"),
            P(),
        ),
        out_specs=(P("ctx", "head", None), P("ctx", None)),
        check_vma=False,
    )
```

```python
import functools
import math

import jax
import jax.numpy as jnp
from jax import lax
from jax.experimental import pallas as pl
from jax.experimental.pallas import tpu as pltpu
from jax.sharding import PartitionSpec as P

HEADS = 64
SCALE_ATTN = 192.0 ** (-0.5)
LOSS_SCALE = 1024.0
NEGATIVE = -1e30
LOG2E = math.log2(math.e)
MESH = pl.DeviceIdType.MESH
F32 = jnp.float32
BF16 = jnp.bfloat16
TOK = 8
STEP = 16
LAG = 1
PIECES = 2
RUN = 64
GROUP = 8
WEIGHTS = (1, 3, 4)
VMEM_LIMIT = 60 * 1024 * 1024


def place(n):
    me = lax.axis_index("ctx")
    a = n // 4
    return me // 4, (me // 2) % 2, me % 2, a


def at(z, x, c):
    return (z * 2 + x) * 2 + c


def remote(src, dst, send, recv, **where):
    return pltpu.make_async_remote_copy(
        src_ref=src, dst_ref=dst, send_sem=send, recv_sem=recv, device_id=where, device_id_type=MESH
    )


def dot_t(a, b):
    return lax.dot_general(a, b, (((1,), (1,)), ((), ())), preferred_element_type=F32)


def gather_kernel(
    n, heads, lat_ref, key_ref, iq_ref, w_ref, lat_out, key_out, idx_ref,
    scr_a, scr_b, send_sem, recv_sem, own_sem,
):
    z, x, c, a = place(n)
    y = lax.axis_index("head")
    other_y = y + 1 - 2 * (y % 2)
    partner = at(z, x, 1 - c)
    rows, depth = key_ref.shape
    part = rows // 2
    mine, others = 1 + y % 2, 2 - y % 2
    me = at(z, x, c)
    owns = []
    for k, (src, dst) in enumerate(((key_ref, key_out), (lat_ref, lat_out))):
        own = pltpu.make_async_copy(src, dst.at[me], own_sem.at[k])
        own.start()
        owns.append(own)

    barrier = pltpu.get_barrier_semaphore()
    greeted = [dict(ctx=at(z, 1 - x, c)), dict(ctx=partner), dict(head=other_y)]
    greeted += [dict(ctx=at(lax.rem(z + d, a), x, c)) for d in range(1, a)]
    for where in greeted:
        pl.semaphore_signal(barrier, inc=1, device_id=where, device_id_type=MESH)
    pl.semaphore_wait(barrier, len(greeted))

    above = a - 1
    spots = dict(
        key_near=0, key_column=0, key_crossed=above, key_core=2 * above + 1,
        near=3 * a - 1, column=3 * a - 1, crossed=3 * a - 1 + above,
        column_rest=3 * a - 1 + 2 * above, crossed_rest=3 * a - 1 + 3 * above,
        core=3 * a + 4 * above,
    )

    def half(ref, k):
        return ref.at[pl.ds(pl.multiple_of((k - 1) * part, part), part)]

    def send(k, slot, spot, d, **where):
        first = slot is me
        if isinstance(k, int) and k == 0:
            src, dst, kind = (key_ref if first else key_out.at[slot]), key_out.at[slot], 0
        else:
            dst, kind = half(lat_out.at[slot], k), 1
            src = half(lat_ref, k) if first else dst
        remote(src, dst, send_sem.at[kind], recv_sem.at[spots[spot] + d], **where).start()

    def to_core(k, slot, d):
        if isinstance(k, int) and k == 0:
            send(k, slot, "key_core", d, ctx=partner)
        else:
            send(k, slot, "core", 0, ctx=partner)

    def to_x(k, slot, spot, d=0):
        send(k, slot, spot, d, ctx=at(z, 1 - x, c))

    def to_y(k, slot, spot, d):
        send(k, slot, spot, d, head=other_y)

    def to_z(k, spot):
        for d in range(1, a):
            send(k, me, spot, d, ctx=at(lax.rem(z + d, a), x, c))

    def arrived(dst, spot, d=0):
        remote(dst, dst, send_sem.at[0], recv_sem.at[spots[spot] + d], ctx=partner).wait_recv()

    def level(d):
        return lax.rem(z + a - d, a)

    def key_near():
        slot = at(z, 1 - x, c)
        arrived(key_out.at[slot], "key_near")
        to_core(0, slot, 0)
        owns[0].wait()
        key_ready(0)

    def key_ready(d):
        arrived(key_out.at[pl.ds(level(d) * 4, 2)], "key_core", d)

    def key_column(d):
        slot = at(level(d), x, c)
        arrived(key_out.at[slot], "key_column", d)
        to_x(0, slot, "key_crossed", d)
        to_core(0, slot, d)

    def key_crossed(d):
        slot = at(level(d), 1 - x, c)
        arrived(key_out.at[slot], "key_crossed", d)
        to_core(0, slot, d)

    def near():
        slot = at(z, 1 - x, c)
        arrived(lat_out.at[slot], "near")
        for k in (mine, others):
            to_core(k, slot, 0)

    def column(d):
        slot = at(level(d), x, c)
        arrived(half(lat_out.at[slot], mine), "column", d)
        to_x(mine, slot, "crossed", d)
        to_y(mine, slot, "column_rest", d)
        to_core(mine, slot, d)

    def crossed(d):
        slot = at(level(d), 1 - x, c)
        arrived(half(lat_out.at[slot], mine), "crossed", d)
        to_y(mine, slot, "crossed_rest", d)
        to_core(mine, slot, d)

    def column_rest(d):
        slot = at(level(d), x, c)
        arrived(half(lat_out.at[slot], others), "column_rest", d)
        to_core(others, slot, d)

    def crossed_rest(d):
        slot = at(level(d), 1 - x, c)
        arrived(half(lat_out.at[slot], others), "crossed_rest", d)
        to_core(others, slot, d)

    to_z(0, "key_column")
    to_x(0, me, "key_near")
    to_core(0, me, 0)
    to_z(mine, "column")
    to_x(mine, me, "near")
    to_x(others, me, "near")
    to_core(mine, me, 0)
    to_core(others, me, 0)

    width = 4 * rows
    m = scr_a.shape[0]
    chunks = iq_ref.shape[0] // m
    steps = chunks * a

    def dots(i, scr):
        r = i % chunks * m
        held = key_out[pl.ds(level(i // chunks) * 4, 4)].reshape(width, depth)
        for h in range(0, m, m // 2):
            scr[h : h + m // 2, :] = dot_t(iq_ref[r + h : r + h + m // 2, :], held)

    def reduce(i, scr):
        first = i % chunks * m
        place_out = pl.ds(pl.multiple_of(level(i // chunks) * width, width), width)
        for t in range(0, m // heads, 8):
            sums = []
            for u in range(t, t + 8):
                total = None
                for g in range(0, heads, 8):
                    r = u * heads + g
                    w = w_ref[first + r : first + r + 8, :]
                    term = jnp.maximum(scr[r : r + 8, :], 0.0) * jnp.concatenate(
                        [w] * (width // 128), axis=1
                    )
                    total = term if total is None else total + term
                sums.append(jnp.sum(total, axis=0, keepdims=True))
            row = first // heads + t
            idx_ref[row : row + 8, place_out] = jnp.concatenate(sums, axis=0)

    events = {}

    def plan(slot, act, *args):
        events.setdefault(slot, []).append(functools.partial(act, *args))

    plan(0, key_near)
    for d in range(1, a):
        plan(1, key_column, d)
    plan(1, near)
    for d in range(1, a):
        plan(1 + d, column, d)
    for d in range(1, a):
        plan(4, key_crossed, d)
        plan(d * chunks // 2, key_ready, d)
        plan(3 + 2 * d, crossed, d)
        plan(4 + 2 * d, column_rest, d)
        plan(6 + 2 * d, crossed_rest, d)
    scrs = (scr_a, scr_b)
    for i in range(steps):
        if i % 2 == 0:
            for act in events.pop(i // 2, ()):
                act()
        dots(i, scrs[i % 2])
        if i > 0:
            reduce(i - 1, scrs[(i - 1) % 2])
    reduce(steps - 1, scrs[(steps - 1) % 2])
    for slot in sorted(events):
        for act in events[slot]:
            act()

    owns[1].wait()
    arrived(lat_out.at[: 2 * a], "core")
    for kind, ref in enumerate((key_out, lat_out)):
        every = ref.at[: n - 1]
        remote(every, every, send_sem.at[kind], recv_sem.at[0], ctx=partner).wait_send()


def gather(latents, keys, iq, wide, heads, n):
    rows = latents.shape[0]
    seq = rows * n
    hbm = pl.BlockSpec(memory_space=pl.ANY)
    vmem = pl.BlockSpec(memory_space=pltpu.VMEM)
    m = STEP * heads
    return pl.pallas_call(
        functools.partial(gather_kernel, n, heads),
        out_shape=(
            jax.ShapeDtypeStruct((n, rows, latents.shape[1]), BF16),
            jax.ShapeDtypeStruct((n, rows, keys.shape[1]), BF16),
            jax.ShapeDtypeStruct((iq.shape[0] // heads, seq), F32),
        ),
        in_specs=[hbm, hbm, vmem, vmem],
        out_specs=(hbm, vmem, vmem),
        scratch_shapes=[
            pltpu.VMEM((m, 4 * rows), F32),
            pltpu.VMEM((m, 4 * rows), F32),
            pltpu.SemaphoreType.DMA((2,)),
            pltpu.SemaphoreType.DMA((7 * (n // 4) - 3,)),
            pltpu.SemaphoreType.DMA((2,)),
        ],
        compiler_params=pltpu.CompilerParams(
            collective_id=0, has_side_effects=True, vmem_limit_bytes=VMEM_LIMIT
        ),
        name="gather",
    )(latents, keys, iq, wide)


def attend_kernel(
    half, n, q_ref, lat_ref, pos_ref, mine_ref, out_ref, low_ref, scr_a, scr_b, top_a, top_b, wide, acc
):
    step = pl.program_id(0)
    seq, depth = lat_ref.shape
    group, _, lanes = q_ref.shape
    count = lanes // 2
    rows = seq // n
    edge = depth // 128 * 128

    @pl.when(step == 0)
    def _():
        lane = lax.broadcasted_iota(jnp.int32, (rows, lanes), 1)
        row = lax.broadcasted_iota(jnp.int32, (rows, lanes), 0)
        own = jnp.where(row <= half * count + lane - (lanes - count), 0.0, NEGATIVE)
        for b in range(n):
            ahead = pos_ref[b] - mine_ref[0]
            bias = jnp.where(ahead == 0, own, jnp.where(ahead < 0, 0.0, NEGATIVE))
            at = slice(b * rows, (b + 1) * rows)
            wide[at, :edge] = lat_ref[at, :edge]
            last = lat_ref[at, edge:].astype(F32)
            last = jnp.concatenate([last, jnp.zeros((rows, lanes - last.shape[1]), F32)], axis=1)
            wide[at, edge:] = jnp.where(lane < depth - edge, last, bias).astype(BF16)
        scr_b[...] = jnp.zeros_like(scr_b)
        top_b[...] = jnp.zeros_like(top_b)
        acc[...] = jnp.zeros_like(acc)

    def scores(first, scr, top_ref):
        def part(h):
            return q_ref[h][:, half * count : (half + 1) * count]

        weights = jnp.concatenate([part(first + h) for h in range(4)], axis=1)
        line = lax.broadcasted_iota(jnp.int32, (count, 4 * count), 0)
        column = lax.broadcasted_iota(jnp.int32, (count, 4 * count), 1)
        same = jnp.where(lax.rem(column, count) == line, 1.0, 0.0).astype(BF16)
        weights = jnp.concatenate([weights, same], axis=0)
        piece = seq // PIECES
        top = None
        for r in range(0, seq, piece):
            v = jnp.dot(wide[r : r + piece, :], weights, preferred_element_type=F32)
            scr[r : r + piece, :] = v
            for k in range(0, piece, 8):
                top = v[k : k + 8] if top is None else jnp.maximum(top, v[k : k + 8])
            yield
        top_ref[...] = top

    def softmax(scr, top_ref, use):
        scale = []
        for tile in (slice(0, lanes), slice(lanes, 2 * lanes)):
            top = jnp.max(top_ref[:, tile], axis=0, keepdims=True)
            total = None
            for r in range(0, seq, RUN):
                p = jnp.exp2((scr[r : r + RUN, tile] - top) * (SCALE_ATTN * LOG2E))
                scr[r : r + RUN, tile] = p
                total = p if total is None else total + p
                yield
            total = jnp.sum(total, axis=0, keepdims=True)
            share = 1.0 / (HEADS * total)
            scale.append(share if use is None else jnp.where(use, share, 0.0))
        for r in range(0, seq, RUN):
            acc[r : r + RUN, :] += (
                scr[r : r + RUN, :lanes] * scale[0] + scr[r : r + RUN, lanes:] * scale[1]
            )
            yield

    def together(dots, vectors):
        total = 3 * (seq // RUN)
        done = 0
        for k, _ in enumerate(dots):
            upto = -(-total * WEIGHTS[k] // WEIGHTS[-1])
            while done < upto:
                next(vectors, None)
                done += 1
        for _ in vectors:
            pass

    for k in range(0, group, 8):
        together(scores(k, scr_a, top_a), softmax(scr_b, top_b, step > 0 if k == 0 else None))
        together(scores(k + 4, scr_b, top_b), softmax(scr_a, top_a, None))

    @pl.when(step == pl.num_programs(0) - 1)
    def _():
        for _ in softmax(scr_b, top_b, None):
            pass
        both = jnp.transpose(acc[...])
        out = both[:count] + both[count:]
        out_ref[...] = out
        low_ref[...] = out.astype(BF16)


def attend(q, lat, block_pos, mine, half, n):
    heads, depth, lanes = q.shape
    seq = lat.shape[0]
    count = lanes // 2
    smem = pl.BlockSpec(memory_space=pltpu.SMEM)
    whole = lambda i: (0, 0)
    return pl.pallas_call(
        functools.partial(attend_kernel, half, n),
        grid=(heads // GROUP,),
        out_shape=(
            jax.ShapeDtypeStruct((count, seq), F32),
            jax.ShapeDtypeStruct((count, seq), BF16),
        ),
        in_specs=[
            pl.BlockSpec((GROUP, depth, lanes), lambda i: (i, 0, 0)),
            pl.BlockSpec((seq, depth), whole),
            smem,
            smem,
        ],
        out_specs=(pl.BlockSpec((count, seq), whole), pl.BlockSpec((count, seq), whole)),
        scratch_shapes=[
            pltpu.VMEM((seq, 2 * lanes), F32),
            pltpu.VMEM((seq, 2 * lanes), F32),
            pltpu.VMEM((8, 2 * lanes), F32),
            pltpu.VMEM((8, 2 * lanes), F32),
            pltpu.VMEM((seq, depth + count), BF16),
            pltpu.VMEM((seq, lanes), F32),
        ],
        compiler_params=pltpu.CompilerParams(vmem_limit_bytes=VMEM_LIMIT),
        cost_estimate=pl.CostEstimate(
            flops=count * heads * seq * depth // 8,
            bytes_accessed=4 * count * heads * depth,
            transcendentals=0,
        ),
        name="attend",
    )(q, lat, block_pos, mine)


def back_kernel(heads, last, iq_ref, w_ref, key_ref, post_ref, poss_ref, *rest):
    peers_i = rest[0]
    own_i, own_t, peers_t = rest[1:4]
    gq_ref, gk_ref, scr, coef, acc, dscr = rest[-6:]
    step = pl.program_id(0)

    @pl.when(step == 0)
    def _():
        acc[...] = rest[4][...] if last else jnp.zeros_like(acc)

    scr[...] = dot_t(iq_ref[...], key_ref[...])
    index, target = own_i[...], own_t[...]
    for k in range(peers_i.shape[0]):
        index = index + peers_i[k]
        target = target + peers_t[k].astype(F32)
    seen = poss_ref[...] <= post_ref[...]
    masked = jnp.where(seen, index, NEGATIVE)
    weights = jnp.where(seen, jnp.exp(masked - jnp.max(masked, axis=1, keepdims=True)), 0.0)
    prob = weights * (1.0 / jnp.sum(weights, axis=1, keepdims=True))
    dscr[...] = jnp.where(seen, LOSS_SCALE * (prob - target), 0.0).astype(BF16).astype(F32)
    for t in range(TOK):
        for g in range(0, heads, 8):
            r = t * heads + g
            wide = jnp.concatenate([w_ref[r : r + 8, :]] * (dscr.shape[1] // 128), axis=1)
            value = dscr[t : t + 1, :] * wide
            coef[r : r + 8, :] = jnp.where(scr[r : r + 8, :] > 0.0, value, 0.0).astype(BF16)
    gq_ref[...] = jnp.dot(coef[...], key_ref[...], preferred_element_type=F32)
    acc[...] += lax.dot_general(
        iq_ref[...], coef[...], (((0,), (0,)), ((), ())), preferred_element_type=F32
    )

    @pl.when(step == pl.num_programs(0) - 1)
    def _():
        if last:
            gk_ref[...] = jnp.transpose(acc[...]).astype(BF16)
        else:
            gk_ref[...] = acc[...]


def back(iq, wide, keys, pos_t, pos_s, peers_i, own_i, own_t, peers_t, carried, heads, first, last):
    depth = iq.shape[1]
    seq = keys.shape[0]
    count = own_t.shape[0]
    m = TOK * heads
    off = first // TOK
    others = peers_i.shape[0]
    return pl.pallas_call(
        functools.partial(back_kernel, heads, last),
        grid=(count // TOK,),
        out_shape=(
            jax.ShapeDtypeStruct(iq.shape, F32),
            jax.ShapeDtypeStruct((seq, depth), BF16)
            if last
            else jax.ShapeDtypeStruct((depth, seq), F32),
        ),
        in_specs=[
            pl.BlockSpec((m, depth), lambda i: (i + off, 0)),
            pl.BlockSpec((m, wide.shape[1]), lambda i: (i + off, 0)),
            pl.BlockSpec((seq, depth), lambda i: (0, 0)),
            pl.BlockSpec((TOK, 1), lambda i: (i + off, 0)),
            pl.BlockSpec((1, seq), lambda i: (0, 0)),
            pl.BlockSpec((others, TOK, seq), lambda i: (0, i + off, 0)),
            pl.BlockSpec((TOK, seq), lambda i: (i + off, 0)),
            pl.BlockSpec((TOK, seq), lambda i: (i, 0)),
            pl.BlockSpec((others, TOK, seq), lambda i: (0, i, 0)),
        ]
        + [pl.BlockSpec((depth, seq), lambda i: (0, 0)), pl.BlockSpec(memory_space=pl.ANY)] * last,
        input_output_aliases={10: 0} if last else {},
        out_specs=(
            pl.BlockSpec((m, depth), lambda i: (i + off, 0)),
            pl.BlockSpec((seq, depth) if last else (depth, seq), lambda i: (0, 0)),
        ),
        scratch_shapes=[
            pltpu.VMEM((m, seq), F32),
            pltpu.VMEM((m, seq), BF16),
            pltpu.VMEM((depth, seq), F32),
            pltpu.VMEM((TOK, seq), F32),
        ],
        compiler_params=pltpu.CompilerParams(vmem_limit_bytes=VMEM_LIMIT),
        cost_estimate=pl.CostEstimate(
            flops=8 * count * heads * seq * depth,
            bytes_accessed=8 * count * heads * depth,
            transcendentals=0,
        ),
        name="back",
    )(iq, wide, keys, pos_t, pos_s, peers_i, own_i, own_t, peers_t, *carried)


def scatter_kernel(
    n, ranks, gk_ref, out_ref, got1, sum1, put2, got2, sum2, put3, got3, put4, got4, ssem, rsem
):
    z, x, c, a = place(n)
    y = lax.axis_index("head")
    barrier = pltpu.get_barrier_semaphore()
    greeted = [dict(ctx=at(z, 1 - x, c)), dict(ctx=at(z, x, 1 - c))]
    greeted += [dict(ctx=at(lax.rem(z + d, a), x, c)) for d in range(1, a)]
    greeted += [dict(head=lax.rem(y + d, ranks)) for d in range(1, ranks)]
    for where in greeted:
        pl.semaphore_signal(barrier, inc=1, device_id=where, device_id_type=MESH)
    pl.semaphore_wait(barrier, len(greeted))

    first = remote(gk_ref.at[:, :, 1 - c], got1, ssem.at[0], rsem.at[0], ctx=at(z, x, 1 - c))
    first.start()
    first.wait()
    sum1[...] = gk_ref[:, :, c].astype(F32) + got1[...].astype(F32)
    put2[...] = sum1[:, 1 - x].astype(BF16)
    second = remote(put2, got2, ssem.at[1], rsem.at[1], ctx=at(z, 1 - x, c))
    second.start()
    second.wait()
    sum2[...] = sum1[:, x] + got2[...].astype(F32)
    put3[...] = sum2[...].astype(BF16)
    third = []
    for d in range(1, a):
        to = lax.rem(z + d, a)
        item = remote(
            put3.at[to], got3.at[d - 1], ssem.at[1 + d], rsem.at[1 + d], ctx=at(to, x, c)
        )
        item.start()
        third.append(item)
    for item in third:
        item.wait()
    part = sum2[z]
    for d in range(1, a):
        part = part + got3[d - 1].astype(F32)
    put4[...] = part
    fourth = []
    for d in range(1, ranks):
        item = remote(
            put4,
            got4.at[d - 1],
            ssem.at[a + d],
            rsem.at[a + d],
            head=lax.rem(y + d, ranks),
        )
        item.start()
        fourth.append(item)
    for item in fourth:
        item.wait()
    part = put4[...]
    for d in range(1, ranks):
        part = part + got4[d - 1]
    out_ref[...] = part


def scatter(gk, n, ranks):
    a = n // 4
    rows, depth = gk.shape[0] // n, gk.shape[1]
    vmem = pl.BlockSpec(memory_space=pltpu.VMEM)
    return pl.pallas_call(
        functools.partial(scatter_kernel, n, ranks),
        out_shape=jax.ShapeDtypeStruct((rows, depth), F32),
        in_specs=[vmem],
        out_specs=vmem,
        scratch_shapes=[
            pltpu.VMEM((a, 2, rows, depth), BF16),
            pltpu.VMEM((a, 2, rows, depth), F32),
            pltpu.VMEM((a, rows, depth), BF16),
            pltpu.VMEM((a, rows, depth), BF16),
            pltpu.VMEM((a, rows, depth), F32),
            pltpu.VMEM((a, rows, depth), BF16),
            pltpu.VMEM((a - 1, rows, depth), BF16),
            pltpu.VMEM((rows, depth), F32),
            pltpu.VMEM((ranks - 1, rows, depth), F32),
            pltpu.SemaphoreType.DMA((a + ranks,)),
            pltpu.SemaphoreType.DMA((a + ranks,)),
        ],
        compiler_params=pltpu.CompilerParams(collective_id=1, has_side_effects=True),
        name="scatter",
    )(gk.reshape(a, 2, 2, rows, depth))


def swap(value, ranks):
    return jnp.stack(
        [
            lax.ppermute(value, "head", [(i, (i + d) % ranks) for i in range(ranks)])
            for d in range(1, ranks)
        ]
    )


def body(queries, latents, index_queries, index_keys, head_weights, block_pos):
    rows, heads, rank = queries.shape
    depth = index_queries.shape[2]
    n, ranks = lax.axis_size("ctx"), lax.axis_size("head")
    seq = rows * n
    q = jnp.transpose(queries, (1, 2, 0))
    iq = index_queries.reshape(rows * heads, depth)
    wide = jnp.broadcast_to(
        (head_weights * depth ** (-0.5))[:, :, None], (rows, heads, 128)
    ).reshape(rows * heads, 128)
    local = jnp.arange(rows, dtype=jnp.int32)
    pos_s = (block_pos[:, None] * rows + local[None, :]).reshape(1, seq)
    mine = jnp.sum(jnp.where(jnp.arange(n) == lax.axis_index("ctx"), block_pos, 0))
    pos_t = (mine * rows + local)[:, None]

    lat, keys, own_i = gather(latents, index_keys, iq, wide, heads, n)
    lat = lat.reshape(seq, rank)
    keys = keys.reshape(seq, depth)
    peers_i = swap(own_i, ranks)
    own_t, peers_t = [], []
    for k in range(2):
        full, low = attend(q, lat, block_pos, mine[None], k, n)
        own_t.append(full)
        peers_t.append(swap(low, ranks))
    grads = ()
    for k in range(2):
        grad_queries, carry = back(
            iq, wide, keys, pos_t, pos_s, peers_i, own_i, own_t[k], peers_t[k], grads, heads,
            k * (rows // 2), k == 1,
        )
        grads = (carry, grad_queries)
    return grad_queries.reshape(rows, heads, depth), scatter(carry, n, ranks)


def solution(mesh):
    return jax.shard_map(
        body,
        mesh=mesh,
        in_specs=(
            P("ctx", "head", None),
            P("ctx", None),
            P("ctx", "head", None),
            P("ctx", None),
            P("ctx", "head"),
            P(),
        ),
        out_specs=(P("ctx", "head", None), P("ctx", None)),
        check_vma=False,
    )
```

```python
import functools
import math

import jax
import jax.numpy as jnp
from jax import lax
from jax.experimental import pallas as pl
from jax.experimental.pallas import tpu as pltpu
from jax.sharding import PartitionSpec as P

HEADS = 64
SCALE_ATTN = 192.0 ** (-0.5)
LOSS_SCALE = 1024.0
NEGATIVE = -1e30
LOG2E = math.log2(math.e)
MESH = pl.DeviceIdType.MESH
F32 = jnp.float32
BF16 = jnp.bfloat16
TOK = 16
STEP = 16
LAG = 1
PIECES = 2
RUN = 64
GROUP = 8
WEIGHTS = (1, 3, 4)
VMEM_LIMIT = 60 * 1024 * 1024


def place(n):
    me = lax.axis_index("ctx")
    a = n // 4
    return me // 4, (me // 2) % 2, me % 2, a


def at(z, x, c):
    return (z * 2 + x) * 2 + c


def remote(src, dst, send, recv, **where):
    return pltpu.make_async_remote_copy(
        src_ref=src, dst_ref=dst, send_sem=send, recv_sem=recv, device_id=where, device_id_type=MESH
    )


def dot_t(a, b):
    return lax.dot_general(a, b, (((1,), (1,)), ((), ())), preferred_element_type=F32)


def gather_kernel(
    n, heads, lat_ref, key_ref, iq_ref, w_ref, lat_out, key_out, idx_ref,
    lat_own, w_scaled, scr_a, scr_b, send_sem, recv_sem, own_sem,
):
    z, x, c, a = place(n)
    y = lax.axis_index("head")
    other_y = y + 1 - 2 * (y % 2)
    partner = at(z, x, 1 - c)
    rows, depth = key_ref.shape
    part = rows // 2
    mine, others = 1 + y % 2, 2 - y % 2
    me = at(z, x, c)
    barrier = pltpu.get_barrier_semaphore()
    greeted = [dict(ctx=at(z, 1 - x, c)), dict(ctx=partner), dict(head=other_y)]
    greeted += [dict(ctx=at(lax.rem(z + d, a), x, c)) for d in range(1, a)]
    for where in greeted:
        pl.semaphore_signal(barrier, inc=1, device_id=where, device_id_type=MESH)
    rank = lat_ref.shape[0]
    for r in range(0, rank, 128):
        end = min(r + 128, rank)
        lat_own[:, r:end] = jnp.transpose(lat_ref[r:end, :].astype(F32)).astype(BF16)
    owns = []
    for k, (src, dst) in enumerate(((key_ref, key_out), (lat_own, lat_out))):
        own = pltpu.make_async_copy(src, dst.at[me], own_sem.at[k])
        own.start()
        owns.append(own)
    w_scaled[...] = w_ref[...] * depth ** (-0.5)
    pl.semaphore_wait(barrier, len(greeted))

    above = a - 1
    spots = dict(
        key_near=0, key_column=0, key_crossed=above, key_core=2 * above + 1,
        near=3 * a - 1, column=3 * a - 1, crossed=3 * a - 1 + above,
        column_rest=3 * a - 1 + 2 * above, crossed_rest=3 * a - 1 + 3 * above,
        core=3 * a + 4 * above,
    )

    def half(ref, k):
        return ref.at[pl.ds(pl.multiple_of((k - 1) * part, part), part)]

    def send(k, slot, spot, d, **where):
        first = slot is me
        if isinstance(k, int) and k == 0:
            src, dst, kind = (key_ref if first else key_out.at[slot]), key_out.at[slot], 0
        else:
            dst, kind = half(lat_out.at[slot], k), 1
            src = half(lat_own, k) if first else dst
        remote(src, dst, send_sem.at[kind], recv_sem.at[spots[spot] + d], **where).start()

    def to_core(k, slot, d):
        if isinstance(k, int) and k == 0:
            send(k, slot, "key_core", d, ctx=partner)
        else:
            send(k, slot, "core", 0, ctx=partner)

    def to_x(k, slot, spot, d=0):
        send(k, slot, spot, d, ctx=at(z, 1 - x, c))

    def to_y(k, slot, spot, d):
        send(k, slot, spot, d, head=other_y)

    def to_z(k, spot):
        for d in range(1, a):
            send(k, me, spot, d, ctx=at(lax.rem(z + d, a), x, c))

    def arrived(dst, spot, d=0):
        remote(dst, dst, send_sem.at[0], recv_sem.at[spots[spot] + d], ctx=partner).wait_recv()

    def level(d):
        return lax.rem(z + a - d, a)

    def key_near():
        slot = at(z, 1 - x, c)
        arrived(key_out.at[slot], "key_near")
        to_core(0, slot, 0)
        owns[0].wait()
        key_ready(0)

    def key_ready(d):
        arrived(key_out.at[pl.ds(level(d) * 4, 2)], "key_core", d)

    def key_column(d):
        slot = at(level(d), x, c)
        arrived(key_out.at[slot], "key_column", d)
        to_x(0, slot, "key_crossed", d)
        to_core(0, slot, d)

    def key_crossed(d):
        slot = at(level(d), 1 - x, c)
        arrived(key_out.at[slot], "key_crossed", d)
        to_core(0, slot, d)

    def near():
        slot = at(z, 1 - x, c)
        arrived(lat_out.at[slot], "near")
        for k in (mine, others):
            to_core(k, slot, 0)

    def column(d):
        slot = at(level(d), x, c)
        arrived(half(lat_out.at[slot], mine), "column", d)
        to_x(mine, slot, "crossed", d)
        to_y(mine, slot, "column_rest", d)
        to_core(mine, slot, d)

    def crossed(d):
        slot = at(level(d), 1 - x, c)
        arrived(half(lat_out.at[slot], mine), "crossed", d)
        to_y(mine, slot, "crossed_rest", d)
        to_core(mine, slot, d)

    def column_rest(d):
        slot = at(level(d), x, c)
        arrived(half(lat_out.at[slot], others), "column_rest", d)
        to_core(others, slot, d)

    def crossed_rest(d):
        slot = at(level(d), 1 - x, c)
        arrived(half(lat_out.at[slot], others), "crossed_rest", d)
        to_core(others, slot, d)

    to_z(0, "key_column")
    to_x(0, me, "key_near")
    to_core(0, me, 0)
    to_z(mine, "column")
    to_x(mine, me, "near")
    to_x(others, me, "near")
    to_core(mine, me, 0)
    to_core(others, me, 0)

    width = 4 * rows
    m = scr_a.shape[0]
    chunks = iq_ref.shape[0] // m
    steps = chunks * a

    def dots(i, scr):
        r = i % chunks * m
        held = key_out[pl.ds(level(i // chunks) * 4, 4)].reshape(width, depth)
        for h in range(0, m, m // 2):
            scr[h : h + m // 2, :] = dot_t(iq_ref[r + h : r + h + m // 2, :], held)

    def reduce(i, scr):
        first = i % chunks * m
        place_out = pl.ds(pl.multiple_of(level(i // chunks) * width, width), width)
        for t in range(0, m // heads, 8):
            sums = []
            for u in range(t, t + 8):
                total = None
                for g in range(0, heads, 8):
                    r = u * heads + g
                    tok = first // heads + u
                    w = jnp.broadcast_to(w_scaled[g : g + 8, tok : tok + 1], (8, width))
                    term = jnp.maximum(scr[r : r + 8, :], 0.0) * w
                    total = term if total is None else total + term
                sums.append(jnp.sum(total, axis=0, keepdims=True))
            row = first // heads + t
            idx_ref[row : row + 8, place_out] = jnp.concatenate(sums, axis=0)

    events = {}

    def plan(slot, act, *args):
        events.setdefault(slot, []).append(functools.partial(act, *args))

    plan(0, key_near)
    for d in range(1, a):
        plan(1, key_column, d)
    plan(1, near)
    for d in range(1, a):
        plan(1 + d, column, d)
    for d in range(1, a):
        plan(4, key_crossed, d)
        plan(d * chunks // 2, key_ready, d)
        plan(3 + 2 * d, crossed, d)
        plan(4 + 2 * d, column_rest, d)
        plan(6 + 2 * d, crossed_rest, d)
    scrs = (scr_a, scr_b)
    for i in range(steps):
        if i % 2 == 0:
            for act in events.pop(i // 2, ()):
                act()
        dots(i, scrs[i % 2])
        if i > 0:
            reduce(i - 1, scrs[(i - 1) % 2])
    reduce(steps - 1, scrs[(steps - 1) % 2])
    for slot in sorted(events):
        for act in events[slot]:
            act()

    owns[1].wait()
    arrived(lat_out.at[: 2 * a], "core")
    for kind, ref in enumerate((key_out, lat_out)):
        every = ref.at[: n - 1]
        remote(every, every, send_sem.at[kind], recv_sem.at[0], ctx=partner).wait_send()


def gather(latents, keys, iq, weights, heads, n):
    rank, rows = latents.shape
    seq = rows * n
    hbm = pl.BlockSpec(memory_space=pl.ANY)
    vmem = pl.BlockSpec(memory_space=pltpu.VMEM)
    m = STEP * heads
    return pl.pallas_call(
        functools.partial(gather_kernel, n, heads),
        out_shape=(
            jax.ShapeDtypeStruct((n, rows, rank), BF16),
            jax.ShapeDtypeStruct((n, rows, keys.shape[1]), BF16),
            jax.ShapeDtypeStruct((iq.shape[0] // heads, seq), F32),
        ),
        in_specs=[vmem, vmem, vmem, vmem],
        out_specs=(hbm, vmem, vmem),
        scratch_shapes=[
            pltpu.VMEM((rows, rank), BF16),
            pltpu.VMEM(weights.shape, F32),
            pltpu.VMEM((m, 4 * rows), F32),
            pltpu.VMEM((m, 4 * rows), F32),
            pltpu.SemaphoreType.DMA((2,)),
            pltpu.SemaphoreType.DMA((7 * (n // 4) - 3,)),
            pltpu.SemaphoreType.DMA((2,)),
        ],
        compiler_params=pltpu.CompilerParams(
            collective_id=0, has_side_effects=True, vmem_limit_bytes=VMEM_LIMIT
        ),
        name="gather",
    )(latents, keys, iq, weights)


def attend_kernel(
    half, n, q_ref, lat_ref, pos_ref, out_ref, low_ref, scr_a, scr_b, top_a, top_b, wide, acc
):
    step = pl.program_id(0)
    seq, depth = lat_ref.shape
    group, _, lanes = q_ref.shape
    count = lanes // 2
    rows = seq // n
    edge = depth // 128 * 128

    @pl.when(step == 0)
    def _():
        lane = lax.broadcasted_iota(jnp.int32, (rows, lanes), 1)
        row = lax.broadcasted_iota(jnp.int32, (rows, lanes), 0)
        own = jnp.where(row <= half * count + lane - (lanes - count), 0.0, NEGATIVE)
        for b in range(n):
            ahead = pos_ref[b] - pos_ref[lax.axis_index("ctx")]
            bias = jnp.where(ahead == 0, own, jnp.where(ahead < 0, 0.0, NEGATIVE))
            at = slice(b * rows, (b + 1) * rows)
            wide[at, :edge] = lat_ref[at, :edge]
            last = lat_ref[at, edge:].astype(F32)
            last = jnp.concatenate([last, jnp.zeros((rows, lanes - last.shape[1]), F32)], axis=1)
            wide[at, edge:] = jnp.where(lane < depth - edge, last, bias).astype(BF16)
        scr_b[...] = jnp.zeros_like(scr_b)
        top_b[...] = jnp.zeros_like(top_b)
        acc[...] = jnp.zeros_like(acc)

    def scores(first, scr, top_ref):
        def part(h):
            return q_ref[h][:, half * count : (half + 1) * count]

        weights = jnp.concatenate([part(first + h) for h in range(4)], axis=1)
        line = lax.broadcasted_iota(jnp.int32, (count, 4 * count), 0)
        column = lax.broadcasted_iota(jnp.int32, (count, 4 * count), 1)
        same = jnp.where(lax.rem(column, count) == line, 1.0, 0.0).astype(BF16)
        weights = jnp.concatenate([weights, same], axis=0)
        piece = seq // PIECES
        top = None
        for r in range(0, seq, piece):
            v = jnp.dot(wide[r : r + piece, :], weights, preferred_element_type=F32)
            scr[r : r + piece, :] = v
            for k in range(0, piece, 8):
                top = v[k : k + 8] if top is None else jnp.maximum(top, v[k : k + 8])
            yield
        top_ref[...] = top

    def softmax(scr, top_ref, use):
        scale = []
        for tile in (slice(0, lanes), slice(lanes, 2 * lanes)):
            top = jnp.max(top_ref[:, tile], axis=0, keepdims=True)
            total = None
            for r in range(0, seq, RUN):
                p = jnp.exp2((scr[r : r + RUN, tile] - top) * (SCALE_ATTN * LOG2E))
                scr[r : r + RUN, tile] = p
                total = p if total is None else total + p
                yield
            total = jnp.sum(total, axis=0, keepdims=True)
            share = 1.0 / (HEADS * total)
            scale.append(share if use is None else jnp.where(use, share, 0.0))
        for r in range(0, seq, RUN):
            acc[r : r + RUN, :] += (
                scr[r : r + RUN, :lanes] * scale[0] + scr[r : r + RUN, lanes:] * scale[1]
            )
            yield

    def together(dots, vectors):
        total = 3 * (seq // RUN)
        done = 0
        for k, _ in enumerate(dots):
            upto = -(-total * WEIGHTS[k] // WEIGHTS[-1])
            while done < upto:
                next(vectors, None)
                done += 1
        for _ in vectors:
            pass

    for k in range(0, group, 8):
        together(scores(k, scr_a, top_a), softmax(scr_b, top_b, step > 0 if k == 0 else None))
        together(scores(k + 4, scr_b, top_b), softmax(scr_a, top_a, None))

    @pl.when(step == pl.num_programs(0) - 1)
    def _():
        for _ in softmax(scr_b, top_b, None):
            pass
        both = jnp.transpose(acc[...])
        out = both[:count] + both[count:]
        out_ref[...] = out
        low_ref[...] = out.astype(BF16)


def attend(q, lat, block_pos, half, n):
    heads, depth, lanes = q.shape
    seq = lat.shape[0]
    count = lanes // 2
    smem = pl.BlockSpec(memory_space=pltpu.SMEM)
    whole = lambda i: (0, 0)
    return pl.pallas_call(
        functools.partial(attend_kernel, half, n),
        grid=(heads // GROUP,),
        out_shape=(
            jax.ShapeDtypeStruct((count, seq), F32),
            jax.ShapeDtypeStruct((count, seq), BF16),
        ),
        in_specs=[
            pl.BlockSpec((GROUP, depth, lanes), lambda i: (i, 0, 0)),
            pl.BlockSpec((seq, depth), whole),
            smem,
        ],
        out_specs=(pl.BlockSpec((count, seq), whole), pl.BlockSpec((count, seq), whole)),
        scratch_shapes=[
            pltpu.VMEM((seq, 2 * lanes), F32),
            pltpu.VMEM((seq, 2 * lanes), F32),
            pltpu.VMEM((8, 2 * lanes), F32),
            pltpu.VMEM((8, 2 * lanes), F32),
            pltpu.VMEM((seq, depth + count), BF16),
            pltpu.VMEM((seq, lanes), F32),
        ],
        compiler_params=pltpu.CompilerParams(vmem_limit_bytes=VMEM_LIMIT),
        cost_estimate=pl.CostEstimate(
            flops=count * heads * seq * depth // 8,
            bytes_accessed=4 * count * heads * depth,
            transcendentals=0,
        ),
        name="attend",
    )(q, lat, block_pos)


def back_kernel(heads, rows, first, last, iq_ref, w_ref, key_ref, pos_ref, *rest):
    peers_i = rest[0]
    own_i, own_t, peers_t = rest[1:4]
    gq_ref, gk_ref, scr, coef, acc, dscr, w_scaled = rest[-7:]
    step = pl.program_id(0)
    start = first + step * TOK
    w_scaled[...] = pltpu.roll(w_ref[...], rows - start, 1) * key_ref.shape[1] ** (-0.5)

    @pl.when(step == 0)
    def _():
        acc[...] = rest[4][...] if last else jnp.zeros_like(acc)

    scr[...] = dot_t(iq_ref[...], key_ref[...])
    index, target = own_i[...], own_t[...]
    for k in range(peers_i.shape[0]):
        index = index + peers_i[k]
        target = target + peers_t[k].astype(F32)
    lane = lax.broadcasted_iota(jnp.int32, (TOK, rows), 1)
    line = lax.broadcasted_iota(jnp.int32, (TOK, rows), 0)
    here = pos_ref[lax.axis_index("ctx")] * rows + start + line - lane
    blocks = key_ref.shape[0] // rows
    ahead = jnp.concatenate([pos_ref[b] * rows - here for b in range(blocks)], axis=1)
    seen = ahead <= 0
    masked = jnp.where(seen, index, NEGATIVE)
    weights = jnp.where(seen, jnp.exp(masked - jnp.max(masked, axis=1, keepdims=True)), 0.0)
    prob = weights * (1.0 / jnp.sum(weights, axis=1, keepdims=True))
    dscr[...] = jnp.where(seen, LOSS_SCALE * (prob - target), 0.0).astype(BF16).astype(F32)
    for t in range(TOK):
        for g in range(0, heads, 8):
            r = t * heads + g
            wide = jnp.broadcast_to(w_scaled[g : g + 8, t : t + 1], (8, dscr.shape[1]))
            value = dscr[t : t + 1, :] * wide
            coef[r : r + 8, :] = jnp.where(scr[r : r + 8, :] > 0.0, value, 0.0).astype(BF16)
    gq_ref[...] = jnp.dot(coef[...], key_ref[...], preferred_element_type=F32)
    acc[...] += lax.dot_general(
        iq_ref[...], coef[...], (((0,), (0,)), ((), ())), preferred_element_type=F32
    )

    @pl.when(step == pl.num_programs(0) - 1)
    def _():
        if last:
            gk_ref[...] = jnp.transpose(acc[...]).astype(BF16)
        else:
            gk_ref[...] = acc[...]


def back(iq, weights, keys, block_pos, peers_i, own_i, own_t, peers_t, carried, heads, first, last):
    depth = iq.shape[1]
    seq = keys.shape[0]
    count = own_t.shape[0]
    m = TOK * heads
    off = first // TOK
    others, rows = peers_i.shape[:2]
    return pl.pallas_call(
        functools.partial(back_kernel, heads, rows, first, last),
        grid=(count // TOK,),
        out_shape=(
            jax.ShapeDtypeStruct(iq.shape, F32),
            jax.ShapeDtypeStruct((seq, depth), BF16)
            if last
            else jax.ShapeDtypeStruct((depth, seq), F32),
        ),
        in_specs=[
            pl.BlockSpec((m, depth), lambda i: (i + off, 0)),
            pl.BlockSpec(weights.shape, lambda i: (0, 0)),
            pl.BlockSpec((seq, depth), lambda i: (0, 0)),
            pl.BlockSpec(memory_space=pltpu.SMEM),
            pl.BlockSpec((others, TOK, seq), lambda i: (0, i + off, 0)),
            pl.BlockSpec((TOK, seq), lambda i: (i + off, 0)),
            pl.BlockSpec((TOK, seq), lambda i: (i, 0)),
            pl.BlockSpec((others, TOK, seq), lambda i: (0, i, 0)),
        ]
        + [pl.BlockSpec((depth, seq), lambda i: (0, 0)), pl.BlockSpec(memory_space=pl.ANY)] * last,
        input_output_aliases={9: 0} if last else {},
        out_specs=(
            pl.BlockSpec((m, depth), lambda i: (i + off, 0)),
            pl.BlockSpec((seq, depth) if last else (depth, seq), lambda i: (0, 0)),
        ),
        scratch_shapes=[
            pltpu.VMEM((m, seq), F32),
            pltpu.VMEM((m, seq), BF16),
            pltpu.VMEM((depth, seq), F32),
            pltpu.VMEM((TOK, seq), F32),
            pltpu.VMEM(weights.shape, F32),
        ],
        compiler_params=pltpu.CompilerParams(vmem_limit_bytes=VMEM_LIMIT),
        cost_estimate=pl.CostEstimate(
            flops=8 * count * heads * seq * depth,
            bytes_accessed=8 * count * heads * depth,
            transcendentals=0,
        ),
        name="back",
    )(iq, weights, keys, block_pos, peers_i, own_i, own_t, peers_t, *carried)


def scatter_kernel(
    n, ranks, gk_ref, put4, got4, got1, sum1, put2, got2, sum2, put3, got3, ssem, rsem
):
    z, x, c, a = place(n)
    y = lax.axis_index("head")
    barrier = pltpu.get_barrier_semaphore()
    greeted = [dict(ctx=at(z, 1 - x, c)), dict(ctx=at(z, x, 1 - c))]
    greeted += [dict(ctx=at(lax.rem(z + d, a), x, c)) for d in range(1, a)]
    greeted += [dict(head=lax.rem(y + d, ranks)) for d in range(1, ranks)]
    for where in greeted:
        pl.semaphore_signal(barrier, inc=1, device_id=where, device_id_type=MESH)
    pl.semaphore_wait(barrier, len(greeted))

    first = remote(gk_ref.at[:, :, 1 - c], got1, ssem.at[0], rsem.at[0], ctx=at(z, x, 1 - c))
    first.start()
    first.wait()
    sum1[...] = gk_ref[:, :, c].astype(F32) + got1[...].astype(F32)
    put2[...] = sum1[:, 1 - x].astype(BF16)
    second = remote(put2, got2, ssem.at[1], rsem.at[1], ctx=at(z, 1 - x, c))
    second.start()
    second.wait()
    sum2[...] = sum1[:, x] + got2[...].astype(F32)
    put3[...] = sum2[...].astype(BF16)
    third = []
    for d in range(1, a):
        to = lax.rem(z + d, a)
        item = remote(
            put3.at[to], got3.at[d - 1], ssem.at[1 + d], rsem.at[1 + d], ctx=at(to, x, c)
        )
        item.start()
        third.append(item)
    for item in third:
        item.wait()
    part = sum2[z]
    for d in range(1, a):
        part = part + got3[d - 1].astype(F32)
    put4[...] = part
    fourth = []
    for d in range(1, ranks):
        item = remote(
            put4,
            got4.at[d - 1],
            ssem.at[a + d],
            rsem.at[a + d],
            head=lax.rem(y + d, ranks),
        )
        item.start()
        fourth.append(item)
    for item in fourth:
        item.wait()


def scatter(gk, n, ranks):
    a = n // 4
    rows, depth = gk.shape[0] // n, gk.shape[1]
    vmem = pl.BlockSpec(memory_space=pltpu.VMEM)
    own, peers = pl.pallas_call(
        functools.partial(scatter_kernel, n, ranks),
        out_shape=(
            jax.ShapeDtypeStruct((rows, depth), F32),
            jax.ShapeDtypeStruct((ranks - 1, rows, depth), F32),
        ),
        in_specs=[vmem],
        out_specs=(vmem, vmem),
        scratch_shapes=[
            pltpu.VMEM((a, 2, rows, depth), BF16),
            pltpu.VMEM((a, 2, rows, depth), F32),
            pltpu.VMEM((a, rows, depth), BF16),
            pltpu.VMEM((a, rows, depth), BF16),
            pltpu.VMEM((a, rows, depth), F32),
            pltpu.VMEM((a, rows, depth), BF16),
            pltpu.VMEM((a - 1, rows, depth), BF16),
            pltpu.SemaphoreType.DMA((a + ranks,)),
            pltpu.SemaphoreType.DMA((a + ranks,)),
        ],
        compiler_params=pltpu.CompilerParams(collective_id=1, has_side_effects=True),
        name="scatter",
    )(gk.reshape(a, 2, 2, rows, depth))
    return own + jnp.sum(peers, axis=0)


def swap(value, ranks):
    return jnp.stack(
        [
            lax.ppermute(value, "head", [(i, (i + d) % ranks) for i in range(ranks)])
            for d in range(1, ranks)
        ]
    )


def body(queries, latents, index_queries, index_keys, head_weights, block_pos):
    rows, heads, rank = queries.shape
    depth = index_queries.shape[2]
    n, ranks = lax.axis_size("ctx"), lax.axis_size("head")
    seq = rows * n
    q = jnp.transpose(queries, (1, 2, 0))
    iq = index_queries.reshape(rows * heads, depth)
    weights = jnp.transpose(head_weights)

    lat, keys, own_i = gather(
        jnp.transpose(latents), index_keys, iq, weights, heads, n
    )
    lat = lat.reshape(seq, rank)
    keys = keys.reshape(seq, depth)
    peers_i = swap(own_i, ranks)
    own_t, peers_t = [], []
    for k in range(2):
        full, low = attend(q, lat, block_pos, k, n)
        own_t.append(full)
        peers_t.append(swap(low, ranks))
    grads = ()
    for k in range(2):
        grad_queries, carry = back(
            iq, weights, keys, block_pos, peers_i, own_i, own_t[k], peers_t[k], grads, heads,
            k * (rows // 2), k == 1,
        )
        grads = (carry, grad_queries)
    return grad_queries.reshape(rows, heads, depth), scatter(carry, n, ranks)


def solution(mesh):
    return jax.shard_map(
        body,
        mesh=mesh,
        in_specs=(
            P("ctx", "head", None),
            P("ctx", None),
            P("ctx", "head", None),
            P("ctx", None),
            P("ctx", "head"),
            P(),
        ),
        out_specs=(P("ctx", "head", None), P("ctx", None)),
        check_vma=False,
    )
```

```python
import functools
import math

import jax
import jax.numpy as jnp
from jax import lax
from jax.experimental import pallas as pl
from jax.experimental.pallas import tpu as pltpu
from jax.sharding import PartitionSpec as P

HEADS = 64
SCALE_ATTN = 192.0 ** (-0.5)
LOSS_SCALE = 1024.0
NEGATIVE = -1e30
LOG2E = math.log2(math.e)
MESH = pl.DeviceIdType.MESH
F32 = jnp.float32
BF16 = jnp.bfloat16
TOK = 16
STEP = 16
LAG = 1
PIECES = 2
RUN = 64
GROUP = 8
WEIGHTS = (1, 3, 4)
VMEM_LIMIT = 60 * 1024 * 1024


def place(n):
    me = lax.axis_index("ctx")
    a = n // 4
    return me // 4, (me // 2) % 2, me % 2, a


def at(z, x, c):
    return (z * 2 + x) * 2 + c


def remote(src, dst, send, recv, **where):
    return pltpu.make_async_remote_copy(
        src_ref=src, dst_ref=dst, send_sem=send, recv_sem=recv, device_id=where, device_id_type=MESH
    )


def dot_t(a, b):
    return lax.dot_general(a, b, (((1,), (1,)), ((), ())), preferred_element_type=F32)


def gather_kernel(
    n, heads, lat_ref, key_ref, iq_ref, w_ref, lat_out, key_out, idx_first, idx_second,
    lat_own, w_scaled, scr_a, scr_b, send_sem, recv_sem, own_sem,
):
    z, x, c, a = place(n)
    y = lax.axis_index("head")
    other_y = y + 1 - 2 * (y % 2)
    partner = at(z, x, 1 - c)
    rows, depth = key_ref.shape
    part = rows // 2
    mine, others = 1 + y % 2, 2 - y % 2
    me = at(z, x, c)
    barrier = pltpu.get_barrier_semaphore()
    greeted = [dict(ctx=at(z, 1 - x, c)), dict(ctx=partner), dict(head=other_y)]
    greeted += [dict(ctx=at(lax.rem(z + d, a), x, c)) for d in range(1, a)]
    for where in greeted:
        pl.semaphore_signal(barrier, inc=1, device_id=where, device_id_type=MESH)
    rank = lat_ref.shape[0]
    for r in range(0, rank, 128):
        end = min(r + 128, rank)
        lat_own[:, r:end] = jnp.transpose(lat_ref[r:end, :].astype(F32)).astype(BF16)
    owns = []
    for k, (src, dst) in enumerate(((key_ref, key_out), (lat_own, lat_out))):
        own = pltpu.make_async_copy(src, dst.at[me], own_sem.at[k])
        own.start()
        owns.append(own)
    w_scaled[...] = w_ref[...] * depth ** (-0.5)
    pl.semaphore_wait(barrier, len(greeted))

    above = a - 1
    spots = dict(
        key_near=0, key_column=0, key_crossed=above, key_core=2 * above + 1,
        near=3 * a - 1, column=3 * a - 1, crossed=3 * a - 1 + above,
        column_rest=3 * a - 1 + 2 * above, crossed_rest=3 * a - 1 + 3 * above,
        core=3 * a + 4 * above,
    )

    def half(ref, k):
        return ref.at[pl.ds(pl.multiple_of((k - 1) * part, part), part)]

    def send(k, slot, spot, d, **where):
        first = slot is me
        if isinstance(k, int) and k == 0:
            src, dst, kind = (key_ref if first else key_out.at[slot]), key_out.at[slot], 0
        else:
            dst, kind = half(lat_out.at[slot], k), 1
            src = half(lat_own, k) if first else dst
        remote(src, dst, send_sem.at[kind], recv_sem.at[spots[spot] + d], **where).start()

    def to_core(k, slot, d):
        if isinstance(k, int) and k == 0:
            send(k, slot, "key_core", d, ctx=partner)
        else:
            send(k, slot, "core", 0, ctx=partner)

    def to_x(k, slot, spot, d=0):
        send(k, slot, spot, d, ctx=at(z, 1 - x, c))

    def to_y(k, slot, spot, d):
        send(k, slot, spot, d, head=other_y)

    def to_z(k, spot):
        for d in range(1, a):
            send(k, me, spot, d, ctx=at(lax.rem(z + d, a), x, c))

    def arrived(dst, spot, d=0):
        remote(dst, dst, send_sem.at[0], recv_sem.at[spots[spot] + d], ctx=partner).wait_recv()

    def level(d):
        return lax.rem(z + a - d, a)

    def key_near():
        slot = at(z, 1 - x, c)
        arrived(key_out.at[slot], "key_near")
        to_core(0, slot, 0)
        owns[0].wait()
        key_ready(0)

    def key_ready(d):
        arrived(key_out.at[pl.ds(level(d) * 4, 2)], "key_core", d)

    def key_column(d):
        slot = at(level(d), x, c)
        arrived(key_out.at[slot], "key_column", d)
        to_x(0, slot, "key_crossed", d)
        to_core(0, slot, d)

    def key_crossed(d):
        slot = at(level(d), 1 - x, c)
        arrived(key_out.at[slot], "key_crossed", d)
        to_core(0, slot, d)

    def near():
        slot = at(z, 1 - x, c)
        arrived(lat_out.at[slot], "near")
        for k in (mine, others):
            to_core(k, slot, 0)

    def column(d):
        slot = at(level(d), x, c)
        arrived(half(lat_out.at[slot], mine), "column", d)
        to_x(mine, slot, "crossed", d)
        to_y(mine, slot, "column_rest", d)
        to_core(mine, slot, d)

    def crossed(d):
        slot = at(level(d), 1 - x, c)
        arrived(half(lat_out.at[slot], mine), "crossed", d)
        to_y(mine, slot, "crossed_rest", d)
        to_core(mine, slot, d)

    def column_rest(d):
        slot = at(level(d), x, c)
        arrived(half(lat_out.at[slot], others), "column_rest", d)
        to_core(others, slot, d)

    def crossed_rest(d):
        slot = at(level(d), 1 - x, c)
        arrived(half(lat_out.at[slot], others), "crossed_rest", d)
        to_core(others, slot, d)

    to_z(0, "key_column")
    to_x(0, me, "key_near")
    to_core(0, me, 0)
    to_z(mine, "column")
    to_x(mine, me, "near")
    to_x(others, me, "near")
    to_core(mine, me, 0)
    to_core(others, me, 0)

    width = 4 * rows
    m = scr_a.shape[0]
    chunks = iq_ref.shape[0] // m
    steps = chunks * a

    def dots(i, scr):
        r = i % chunks * m
        held = key_out[pl.ds(level(i // chunks) * 4, 4)].reshape(width, depth)
        for h in range(0, m, m // 2):
            scr[h : h + m // 2, :] = dot_t(iq_ref[r + h : r + h + m // 2, :], held)

    def reduce(i, scr):
        first = i % chunks * m
        place_out = pl.ds(pl.multiple_of(level(i // chunks) * width, width), width)
        for t in range(0, m // heads, 8):
            sums = []
            for u in range(t, t + 8):
                total = None
                for g in range(0, heads, 8):
                    r = u * heads + g
                    tok = first // heads + u
                    w = jnp.broadcast_to(w_scaled[g : g + 8, tok : tok + 1], (8, width))
                    term = jnp.maximum(scr[r : r + 8, :], 0.0) * w
                    total = term if total is None else total + term
                sums.append(jnp.sum(total, axis=0, keepdims=True))
            row = first // heads + t
            idx_ref, row = (idx_first, row) if row < part else (idx_second, row - part)
            idx_ref[row : row + 8, place_out] = jnp.concatenate(sums, axis=0)

    events = {}

    def plan(slot, act, *args):
        events.setdefault(slot, []).append(functools.partial(act, *args))

    plan(0, key_near)
    for d in range(1, a):
        plan(1, key_column, d)
    plan(1, near)
    for d in range(1, a):
        plan(1 + d, column, d)
    for d in range(1, a):
        plan(4, key_crossed, d)
        plan(d * chunks // 2, key_ready, d)
        plan(3 + 2 * d, crossed, d)
        plan(4 + 2 * d, column_rest, d)
        plan(6 + 2 * d, crossed_rest, d)
    scrs = (scr_a, scr_b)
    for i in range(steps):
        if i % 2 == 0:
            for act in events.pop(i // 2, ()):
                act()
        dots(i, scrs[i % 2])
        if i > 0:
            reduce(i - 1, scrs[(i - 1) % 2])
    reduce(steps - 1, scrs[(steps - 1) % 2])
    for slot in sorted(events):
        for act in events[slot]:
            act()

    owns[1].wait()
    arrived(lat_out.at[: 2 * a], "core")
    for kind, ref in enumerate((key_out, lat_out)):
        every = ref.at[: n - 1]
        remote(every, every, send_sem.at[kind], recv_sem.at[0], ctx=partner).wait_send()


def gather(latents, keys, iq, weights, heads, n):
    rank, rows = latents.shape
    seq = rows * n
    hbm = pl.BlockSpec(memory_space=pl.ANY)
    vmem = pl.BlockSpec(memory_space=pltpu.VMEM)
    m = STEP * heads
    return pl.pallas_call(
        functools.partial(gather_kernel, n, heads),
        out_shape=(
            jax.ShapeDtypeStruct((n, rows, rank), BF16),
            jax.ShapeDtypeStruct((n, rows, keys.shape[1]), BF16),
            jax.ShapeDtypeStruct((rows // 2, seq), F32),
            jax.ShapeDtypeStruct((rows // 2, seq), F32),
        ),
        in_specs=[vmem, vmem, vmem, vmem],
        out_specs=(hbm, vmem, vmem, vmem),
        scratch_shapes=[
            pltpu.VMEM((rows, rank), BF16),
            pltpu.VMEM(weights.shape, F32),
            pltpu.VMEM((m, 4 * rows), F32),
            pltpu.VMEM((m, 4 * rows), F32),
            pltpu.SemaphoreType.DMA((2,)),
            pltpu.SemaphoreType.DMA((7 * (n // 4) - 3,)),
            pltpu.SemaphoreType.DMA((2,)),
        ],
        compiler_params=pltpu.CompilerParams(
            collective_id=0, has_side_effects=True, vmem_limit_bytes=VMEM_LIMIT
        ),
        name="gather",
    )(latents, keys, iq, weights)


def attend_kernel(
    half, n, q_ref, lat_ref, pos_ref, out_ref, low_ref, scr_a, scr_b, top_a, top_b, wide, acc
):
    step = pl.program_id(0)
    seq, depth = lat_ref.shape
    group, _, lanes = q_ref.shape
    count = lanes // 2
    rows = seq // n
    edge = depth // 128 * 128

    @pl.when(step == 0)
    def _():
        lane = lax.broadcasted_iota(jnp.int32, (rows, lanes), 1)
        row = lax.broadcasted_iota(jnp.int32, (rows, lanes), 0)
        own = jnp.where(row <= half * count + lane - (lanes - count), 0.0, NEGATIVE)
        for b in range(n):
            ahead = pos_ref[b] - pos_ref[lax.axis_index("ctx")]
            bias = jnp.where(ahead == 0, own, jnp.where(ahead < 0, 0.0, NEGATIVE))
            at = slice(b * rows, (b + 1) * rows)
            wide[at, :edge] = lat_ref[at, :edge]
            last = lat_ref[at, edge:].astype(F32)
            last = jnp.concatenate([last, jnp.zeros((rows, lanes - last.shape[1]), F32)], axis=1)
            wide[at, edge:] = jnp.where(lane < depth - edge, last, bias).astype(BF16)
        scr_b[...] = jnp.zeros_like(scr_b)
        top_b[...] = jnp.zeros_like(top_b)
        acc[...] = jnp.zeros_like(acc)

    def scores(first, scr, top_ref):
        def part(h):
            return q_ref[h][:, half * count : (half + 1) * count]

        weights = jnp.concatenate([part(first + h) for h in range(4)], axis=1)
        line = lax.broadcasted_iota(jnp.int32, (count, 4 * count), 0)
        column = lax.broadcasted_iota(jnp.int32, (count, 4 * count), 1)
        same = jnp.where(lax.rem(column, count) == line, 1.0, 0.0).astype(BF16)
        weights = jnp.concatenate([weights, same], axis=0)
        piece = seq // PIECES
        top = None
        for r in range(0, seq, piece):
            v = jnp.dot(wide[r : r + piece, :], weights, preferred_element_type=F32)
            scr[r : r + piece, :] = v
            for k in range(0, piece, 8):
                top = v[k : k + 8] if top is None else jnp.maximum(top, v[k : k + 8])
            yield
        top_ref[...] = top

    def softmax(scr, top_ref, use):
        scale = []
        for tile in (slice(0, lanes), slice(lanes, 2 * lanes)):
            top = jnp.max(top_ref[:, tile], axis=0, keepdims=True)
            total = None
            for r in range(0, seq, RUN):
                p = jnp.exp2((scr[r : r + RUN, tile] - top) * (SCALE_ATTN * LOG2E))
                scr[r : r + RUN, tile] = p
                total = p if total is None else total + p
                yield
            total = jnp.sum(total, axis=0, keepdims=True)
            share = 1.0 / (HEADS * total)
            scale.append(share if use is None else jnp.where(use, share, 0.0))
        for r in range(0, seq, RUN):
            acc[r : r + RUN, :] += (
                scr[r : r + RUN, :lanes] * scale[0] + scr[r : r + RUN, lanes:] * scale[1]
            )
            yield

    def together(dots, vectors):
        total = 3 * (seq // RUN)
        done = 0
        for k, _ in enumerate(dots):
            upto = -(-total * WEIGHTS[k] // WEIGHTS[-1])
            while done < upto:
                next(vectors, None)
                done += 1
        for _ in vectors:
            pass

    for k in range(0, group, 8):
        together(scores(k, scr_a, top_a), softmax(scr_b, top_b, step > 0 if k == 0 else None))
        together(scores(k + 4, scr_b, top_b), softmax(scr_a, top_a, None))

    @pl.when(step == pl.num_programs(0) - 1)
    def _():
        for _ in softmax(scr_b, top_b, None):
            pass
        both = jnp.transpose(acc[...])
        out = both[:count] + both[count:]
        out_ref[...] = out
        low_ref[...] = out.astype(BF16)


def attend(q, lat, block_pos, half, n):
    heads, depth, lanes = q.shape
    seq = lat.shape[0]
    count = lanes // 2
    smem = pl.BlockSpec(memory_space=pltpu.SMEM)
    whole = lambda i: (0, 0)
    return pl.pallas_call(
        functools.partial(attend_kernel, half, n),
        grid=(heads // GROUP,),
        out_shape=(
            jax.ShapeDtypeStruct((count, seq), F32),
            jax.ShapeDtypeStruct((count, seq), BF16),
        ),
        in_specs=[
            pl.BlockSpec((GROUP, depth, lanes), lambda i: (i, 0, 0)),
            pl.BlockSpec((seq, depth), whole),
            smem,
        ],
        out_specs=(pl.BlockSpec((count, seq), whole), pl.BlockSpec((count, seq), whole)),
        scratch_shapes=[
            pltpu.VMEM((seq, 2 * lanes), F32),
            pltpu.VMEM((seq, 2 * lanes), F32),
            pltpu.VMEM((8, 2 * lanes), F32),
            pltpu.VMEM((8, 2 * lanes), F32),
            pltpu.VMEM((seq, depth + count), BF16),
            pltpu.VMEM((seq, lanes), F32),
        ],
        compiler_params=pltpu.CompilerParams(vmem_limit_bytes=VMEM_LIMIT),
        cost_estimate=pl.CostEstimate(
            flops=count * heads * seq * depth // 8,
            bytes_accessed=4 * count * heads * depth,
            transcendentals=0,
        ),
        name="attend",
    )(q, lat, block_pos)


def delta_rows(index, target, pos_ref, start, rows):
    count, seq = index.shape
    lane = lax.broadcasted_iota(jnp.int32, (count, rows), 1)
    line = lax.broadcasted_iota(jnp.int32, (count, rows), 0)
    here = pos_ref[lax.axis_index("ctx")] * rows + start + line - lane
    ahead = jnp.concatenate([pos_ref[b] * rows - here for b in range(seq // rows)], axis=1)
    seen = ahead <= 0
    masked = jnp.where(seen, index, NEGATIVE)
    weights = jnp.where(seen, jnp.exp(masked - jnp.max(masked, axis=1, keepdims=True)), 0.0)
    prob = weights * (1.0 / jnp.sum(weights, axis=1, keepdims=True))
    return jnp.where(seen, LOSS_SCALE * (prob - target), 0.0).astype(BF16).astype(F32)


def back_kernel(
    heads, rows, iq_ref, w_ref, key_ref, pos_ref, peers_i, own_i, own_t, peers_t,
    gq_ref, gk_ref, scr, coef, dscr, w_scaled,
):
    step = pl.program_id(0)
    start = step * TOK
    w_scaled[...] = pltpu.roll(w_ref[...], rows - start, 1) * key_ref.shape[1] ** (-0.5)

    @pl.when(step == 0)
    def _():
        gk_ref[...] = jnp.zeros_like(gk_ref)

    scr[...] = dot_t(iq_ref[...], key_ref[...])
    index, target = own_i[...], own_t[...]
    for k in range(peers_i.shape[0]):
        index = index + peers_i[k]
        target = target + peers_t[k].astype(F32)
    dscr[...] = delta_rows(index, target, pos_ref, start, rows)
    for t in range(TOK):
        for g in range(0, heads, 8):
            r = t * heads + g
            wide = jnp.broadcast_to(w_scaled[g : g + 8, t : t + 1], (8, dscr.shape[1]))
            value = dscr[t : t + 1, :] * wide
            coef[r : r + 8, :] = jnp.where(scr[r : r + 8, :] > 0.0, value, 0.0).astype(BF16)
    gq_ref[...] = jnp.dot(coef[...], key_ref[...], preferred_element_type=F32)
    gk_ref[...] += lax.dot_general(
        iq_ref[...], coef[...], (((0,), (0,)), ((), ())), preferred_element_type=F32
    )


def back(iq, weights, keys, block_pos, peers_i, own_i, own_t, peers_t, heads):
    depth = iq.shape[1]
    rows = weights.shape[1]
    count, seq = own_t.shape
    m = TOK * heads
    others = peers_i.shape[0]
    return pl.pallas_call(
        functools.partial(back_kernel, heads, rows),
        grid=(count // TOK,),
        out_shape=(
            jax.ShapeDtypeStruct((count * heads, depth), F32),
            jax.ShapeDtypeStruct((depth, seq), F32),
        ),
        in_specs=[
            pl.BlockSpec((m, depth), lambda i: (i, 0)),
            pl.BlockSpec(weights.shape, lambda i: (0, 0)),
            pl.BlockSpec((seq, depth), lambda i: (0, 0)),
            pl.BlockSpec(memory_space=pltpu.SMEM),
            pl.BlockSpec((others, TOK, seq), lambda i: (0, i, 0)),
            pl.BlockSpec((TOK, seq), lambda i: (i, 0)),
            pl.BlockSpec((TOK, seq), lambda i: (i, 0)),
            pl.BlockSpec((others, TOK, seq), lambda i: (0, i, 0)),
        ],
        out_specs=(
            pl.BlockSpec((m, depth), lambda i: (i, 0)),
            pl.BlockSpec((depth, seq), lambda i: (0, 0)),
        ),
        scratch_shapes=[
            pltpu.VMEM((m, seq), F32),
            pltpu.VMEM((m, seq), BF16),
            pltpu.VMEM((TOK, seq), F32),
            pltpu.VMEM(weights.shape, F32),
        ],
        compiler_params=pltpu.CompilerParams(vmem_limit_bytes=VMEM_LIMIT),
        cost_estimate=pl.CostEstimate(
            flops=8 * count * heads * seq * depth,
            bytes_accessed=8 * count * heads * depth,
            transcendentals=0,
        ),
        name="back",
    )(iq, weights, keys, block_pos, peers_i, own_i, own_t, peers_t)


def finish_kernel(
    n, heads, ranks, iq_ref, w_ref, key_ref, pos_ref, peers_i, own_i, own_t, peers_t, carried,
    gq_ref, put4, got4, scr, coef, dscr, w_scaled, acc,
    sum0, put1, got1, sum1, put2, got2, put3, got3, ssem, rsem,
):
    z, x, c, a = place(n)
    y = lax.axis_index("head")
    barrier = pltpu.get_barrier_semaphore()
    greeted = [dict(ctx=at(z, 1 - x, c)), dict(ctx=at(z, x, 1 - c))]
    greeted += [dict(ctx=at(lax.rem(z + d, a), x, c)) for d in range(1, a)]
    greeted += [dict(head=lax.rem(y + d, ranks)) for d in range(1, ranks)]
    for where in greeted:
        pl.semaphore_signal(barrier, inc=1, device_id=where, device_id_type=MESH)

    depth = key_ref.shape[1]
    count, seq = own_t.shape
    rows = w_ref.shape[1]
    width = 4 * rows
    m = TOK * heads
    w_scaled[...] = w_ref[...] * depth ** (-0.5)
    for t in range(0, count, TOK):
        span = slice(t, t + TOK)
        index, target = own_i[span, :], own_t[span, :]
        for k in range(ranks - 1):
            index = index + peers_i[k, span, :]
            target = target + peers_t[k, span, :].astype(F32)
        dscr[span, :] = delta_rows(index, target, pos_ref, rows - count + t, rows)

    order = [*range(1, a), 0]

    def copy(stage, e, src, dst, **where):
        k = stage * a + e
        return remote(src, dst, ssem.at[k], rsem.at[k], **where)

    def core(e):
        return copy(0, e, put1.at[e], got1.at[e], ctx=at(z, x, 1 - c))

    def side(e):
        return copy(1, e, put2.at[e], got2.at[e], ctx=at(z, 1 - x, c))

    def line(e):
        to = lax.rem(z + order[e], a)
        return copy(2, e, put3.at[e], got3.at[e], ctx=at(to, x, c))

    def compute(e):
        zd = lax.rem(z + order[e], a)
        cols = pl.ds(pl.multiple_of(zd * width, width), width)
        held = key_ref[cols, :]
        acc[...] = carried[:, cols]
        for t in range(0, count, TOK):
            part = slice(t * heads, t * heads + m)
            iq = iq_ref[part, :]
            scr[...] = dot_t(iq, held)
            for u in range(TOK):
                row = dscr[t + u : t + u + 1, cols]
                tok = rows - count + t + u
                for g in range(0, heads, 8):
                    r = u * heads + g
                    wide = jnp.broadcast_to(w_scaled[g : g + 8, tok : tok + 1], (8, width))
                    coef[r : r + 8, :] = jnp.where(
                        scr[r : r + 8, :] > 0.0, row * wide, 0.0
                    ).astype(BF16)
            grad = jnp.dot(coef[...], held, preferred_element_type=F32)
            gq_ref[part, :] = grad if e == 0 else gq_ref[part, :] + grad
            acc[...] += lax.dot_general(
                iq, coef[...], (((0,), (0,)), ((), ())), preferred_element_type=F32
            )
        sum0[e] = jnp.transpose(acc[...]).reshape(2, 2, rows, depth)

    def first(e):
        put1[e] = sum0[e, :, 1 - c].astype(BF16)
        core(e).start()

    def second(e):
        core(e).wait_recv()
        sum1[e] = sum0[e, x, c] + got1[e, x].astype(F32)
        put2[e] = (sum0[e, 1 - x, c] + got1[e, 1 - x].astype(F32)).astype(BF16)
        side(e).start()

    def third(e):
        side(e).wait_recv()
        total = sum1[e] + got2[e].astype(F32)
        if e < a - 1:
            put3[e] = total.astype(BF16)
            line(e).start()
        else:
            for k in range(a - 1):
                line(k).wait_recv()
                total = total + got3[k].astype(F32)
            put4[...] = total

    for e in range(a):
        compute(e)
        if e == 0:
            pl.semaphore_wait(barrier, len(greeted))
        first(e)
        if e > 0:
            second(e - 1)
        if e > 1:
            third(e - 2)
    second(a - 1)
    third(a - 2)
    third(a - 1)
    last = []
    for d in range(1, ranks):
        item = remote(
            put4, got4.at[d - 1], ssem.at[3 * a + d - 1], rsem.at[3 * a + d - 1],
            head=lax.rem(y + d, ranks),
        )
        item.start()
        last.append(item)
    for e in range(a):
        core(e).wait_send()
        side(e).wait_send()
        if e < a - 1:
            line(e).wait_send()
    for item in last:
        item.wait()


def finish(iq, weights, keys, block_pos, peers_i, own_i, own_t, peers_t, carried, heads, n, ranks):
    depth = iq.shape[1]
    rows = weights.shape[1]
    count, seq = own_t.shape
    half = count * heads
    m = TOK * heads
    a = n // 4
    vmem = pl.BlockSpec(memory_space=pltpu.VMEM)
    grad, own, peers = pl.pallas_call(
        functools.partial(finish_kernel, n, heads, ranks),
        grid=(1,),
        out_shape=(
            jax.ShapeDtypeStruct((half, depth), F32),
            jax.ShapeDtypeStruct((rows, depth), F32),
            jax.ShapeDtypeStruct((ranks - 1, rows, depth), F32),
        ),
        in_specs=[
            pl.BlockSpec((half, depth), lambda i: (1, 0)),
            vmem, vmem, pl.BlockSpec(memory_space=pltpu.SMEM), vmem, vmem, vmem, vmem, vmem,
        ],
        out_specs=(vmem, vmem, vmem),
        scratch_shapes=[
            pltpu.VMEM((m, 4 * rows), F32),
            pltpu.VMEM((m, 4 * rows), BF16),
            pltpu.VMEM((count, seq), F32),
            pltpu.VMEM(weights.shape, F32),
            pltpu.VMEM((depth, 4 * rows), F32),
            pltpu.VMEM((a, 2, 2, rows, depth), F32),
            pltpu.VMEM((a, 2, rows, depth), BF16),
            pltpu.VMEM((a, 2, rows, depth), BF16),
            pltpu.VMEM((a, rows, depth), F32),
            pltpu.VMEM((a, rows, depth), BF16),
            pltpu.VMEM((a, rows, depth), BF16),
            pltpu.VMEM((a, rows, depth), BF16),
            pltpu.VMEM((a, rows, depth), BF16),
            pltpu.SemaphoreType.DMA((3 * a + ranks - 1,)),
            pltpu.SemaphoreType.DMA((3 * a + ranks - 1,)),
        ],
        compiler_params=pltpu.CompilerParams(
            collective_id=1, has_side_effects=True, vmem_limit_bytes=VMEM_LIMIT
        ),
        name="finish",
    )(iq, weights, keys, block_pos, peers_i, own_i, own_t, peers_t, carried)
    return grad, own + jnp.sum(peers, axis=0)


def swap(value, ranks):
    return jnp.stack(
        [
            lax.ppermute(value, "head", [(i, (i + d) % ranks) for i in range(ranks)])
            for d in range(1, ranks)
        ]
    )


def body(queries, latents, index_queries, index_keys, head_weights, block_pos):
    rows, heads, rank = queries.shape
    depth = index_queries.shape[2]
    n, ranks = lax.axis_size("ctx"), lax.axis_size("head")
    seq = rows * n
    q = jnp.transpose(queries, (1, 2, 0))
    iq = index_queries.reshape(rows * heads, depth)
    weights = jnp.transpose(head_weights)

    lat, keys, *own_i = gather(jnp.transpose(latents), index_keys, iq, weights, heads, n)
    lat = lat.reshape(seq, rank)
    keys = keys.reshape(seq, depth)
    peers_i = [swap(value, ranks) for value in own_i]
    own_t, peers_t = [], []
    for k in range(2):
        full, low = attend(q, lat, block_pos, k, n)
        own_t.append(full)
        peers_t.append(swap(low, ranks))
    first, carried = back(
        iq, weights, keys, block_pos, peers_i[0], own_i[0], own_t[0], peers_t[0], heads
    )
    second, grad_keys = finish(
        iq, weights, keys, block_pos, peers_i[1], own_i[1], own_t[1], peers_t[1], carried, heads,
        n, ranks,
    )
    return jnp.concatenate([first, second]).reshape(rows, heads, depth), grad_keys


def solution(mesh):
    return jax.shard_map(
        body,
        mesh=mesh,
        in_specs=(
            P("ctx", "head", None),
            P("ctx", None),
            P("ctx", "head", None),
            P("ctx", None),
            P("ctx", "head"),
            P(),
        ),
        out_specs=(P("ctx", "head", None), P("ctx", None)),
        check_vma=False,
    )
```

```python
import functools
import math

import jax
import jax.numpy as jnp
from jax import lax
from jax.experimental import pallas as pl
from jax.experimental.pallas import tpu as pltpu
from jax.sharding import PartitionSpec as P

HEADS = 64
SCALE_ATTN = 192.0 ** (-0.5)
LOSS_SCALE = 1024.0
NEGATIVE = -1e30
LOG2E = math.log2(math.e)
MESH = pl.DeviceIdType.MESH
F32 = jnp.float32
BF16 = jnp.bfloat16
TOK = 16
STEP = 16
LAG = 1
PIECES = 2
RUN = 64
GROUP = 8
WEIGHTS = (1, 3, 4)
VMEM_LIMIT = 60 * 1024 * 1024


def place(n):
    me = lax.axis_index("ctx")
    a = n // 4
    return me // 4, (me // 2) % 2, me % 2, a


def at(z, x, c):
    return (z * 2 + x) * 2 + c


def remote(src, dst, send, recv, **where):
    return pltpu.make_async_remote_copy(
        src_ref=src, dst_ref=dst, send_sem=send, recv_sem=recv, device_id=where, device_id_type=MESH
    )


def dot_t(a, b):
    return lax.dot_general(a, b, (((1,), (1,)), ((), ())), preferred_element_type=F32)


def gather_kernel(
    n, heads, lat_ref, key_ref, iq_ref, w_ref, lat_out, key_out, idx_first, idx_second,
    lat_own, w_scaled, scr_a, scr_b, send_sem, recv_sem, own_sem,
):
    z, x, c, a = place(n)
    y = lax.axis_index("head")
    other_y = y + 1 - 2 * (y % 2)
    partner = at(z, x, 1 - c)
    rows, depth = key_ref.shape
    part = rows // 2
    mine, others = 1 + y % 2, 2 - y % 2
    me = at(z, x, c)
    barrier = pltpu.get_barrier_semaphore()
    greeted = [dict(ctx=at(z, 1 - x, c)), dict(ctx=partner), dict(head=other_y)]
    greeted += [dict(ctx=at(lax.rem(z + d, a), x, c)) for d in range(1, a)]
    for where in greeted:
        pl.semaphore_signal(barrier, inc=1, device_id=where, device_id_type=MESH)
    rank = lat_ref.shape[0]
    for r in range(0, rank, 128):
        end = min(r + 128, rank)
        lat_own[:, r:end] = jnp.transpose(lat_ref[r:end, :].astype(F32)).astype(BF16)
    owns = []
    for k, (src, dst) in enumerate(((key_ref, key_out), (lat_own, lat_out))):
        own = pltpu.make_async_copy(src, dst.at[me], own_sem.at[k])
        own.start()
        owns.append(own)
    w_scaled[...] = w_ref[...] * depth ** (-0.5)
    pl.semaphore_wait(barrier, len(greeted))

    above = a - 1
    spots = dict(
        key_near=0, key_column=0, key_crossed=above, key_core=2 * above + 1,
        near=3 * a - 1, column=3 * a - 1, crossed=3 * a - 1 + above,
        column_rest=3 * a - 1 + 2 * above, crossed_rest=3 * a - 1 + 3 * above,
        core=3 * a + 4 * above,
    )

    def half(ref, k):
        return ref.at[pl.ds(pl.multiple_of((k - 1) * part, part), part)]

    def send(k, slot, spot, d, **where):
        first = slot is me
        if isinstance(k, int) and k == 0:
            src, dst, kind = (key_ref if first else key_out.at[slot]), key_out.at[slot], 0
        else:
            dst, kind = half(lat_out.at[slot], k), 1
            src = half(lat_own, k) if first else dst
        remote(src, dst, send_sem.at[kind], recv_sem.at[spots[spot] + d], **where).start()

    def to_core(k, slot, d):
        if isinstance(k, int) and k == 0:
            send(k, slot, "key_core", d, ctx=partner)
        else:
            send(k, slot, "core", 0, ctx=partner)

    def to_x(k, slot, spot, d=0):
        send(k, slot, spot, d, ctx=at(z, 1 - x, c))

    def to_y(k, slot, spot, d):
        send(k, slot, spot, d, head=other_y)

    def to_z(k, spot):
        for d in range(1, a):
            send(k, me, spot, d, ctx=at(lax.rem(z + d, a), x, c))

    def arrived(dst, spot, d=0):
        remote(dst, dst, send_sem.at[0], recv_sem.at[spots[spot] + d], ctx=partner).wait_recv()

    def level(d):
        return lax.rem(z + a - d, a)

    def key_near():
        slot = at(z, 1 - x, c)
        arrived(key_out.at[slot], "key_near")
        to_core(0, slot, 0)
        owns[0].wait()
        key_ready(0)

    def key_ready(d):
        arrived(key_out.at[pl.ds(level(d) * 4, 2)], "key_core", d)

    def key_column(d):
        slot = at(level(d), x, c)
        arrived(key_out.at[slot], "key_column", d)
        to_x(0, slot, "key_crossed", d)
        to_core(0, slot, d)

    def key_crossed(d):
        slot = at(level(d), 1 - x, c)
        arrived(key_out.at[slot], "key_crossed", d)
        to_core(0, slot, d)

    def near():
        slot = at(z, 1 - x, c)
        arrived(lat_out.at[slot], "near")
        for k in (mine, others):
            to_core(k, slot, 0)

    def column(d):
        slot = at(level(d), x, c)
        arrived(half(lat_out.at[slot], mine), "column", d)
        to_x(mine, slot, "crossed", d)
        to_y(mine, slot, "column_rest", d)
        to_core(mine, slot, d)

    def crossed(d):
        slot = at(level(d), 1 - x, c)
        arrived(half(lat_out.at[slot], mine), "crossed", d)
        to_y(mine, slot, "crossed_rest", d)
        to_core(mine, slot, d)

    def column_rest(d):
        slot = at(level(d), x, c)
        arrived(half(lat_out.at[slot], others), "column_rest", d)
        to_core(others, slot, d)

    def crossed_rest(d):
        slot = at(level(d), 1 - x, c)
        arrived(half(lat_out.at[slot], others), "crossed_rest", d)
        to_core(others, slot, d)

    to_z(0, "key_column")
    to_x(0, me, "key_near")
    to_core(0, me, 0)
    to_z(mine, "column")
    to_x(mine, me, "near")
    to_x(others, me, "near")
    to_core(mine, me, 0)
    to_core(others, me, 0)

    width = 4 * rows
    m = scr_a.shape[0]
    chunks = iq_ref.shape[0] // m
    steps = chunks * a

    def dots(i, scr):
        r = i % chunks * m
        held = key_out[pl.ds(level(i // chunks) * 4, 4)].reshape(width, depth)
        for h in range(0, m, m // 2):
            scr[h : h + m // 2, :] = dot_t(iq_ref[r + h : r + h + m // 2, :], held)

    def reduce(i, scr):
        first = i % chunks * m
        place_out = pl.ds(pl.multiple_of(level(i // chunks) * width, width), width)
        for t in range(0, m // heads, 8):
            sums = []
            for u in range(t, t + 8):
                total = None
                for g in range(0, heads, 8):
                    r = u * heads + g
                    tok = first // heads + u
                    w = jnp.broadcast_to(w_scaled[g : g + 8, tok : tok + 1], (8, width))
                    term = jnp.maximum(scr[r : r + 8, :], 0.0) * w
                    total = term if total is None else total + term
                sums.append(jnp.sum(total, axis=0, keepdims=True))
            row = first // heads + t
            idx_ref, row = (idx_first, row) if row < part else (idx_second, row - part)
            idx_ref[row : row + 8, place_out] = jnp.concatenate(sums, axis=0)

    events = {}

    def plan(slot, act, *args):
        events.setdefault(slot, []).append(functools.partial(act, *args))

    plan(0, key_near)
    for d in range(1, a):
        plan(1, key_column, d)
    plan(1, near)
    for d in range(1, a):
        plan(1 + d, column, d)
    for d in range(1, a):
        plan(4, key_crossed, d)
        plan(d * chunks // 2, key_ready, d)
        plan(3 + 2 * d, crossed, d)
        plan(4 + 2 * d, column_rest, d)
        plan(6 + 2 * d, crossed_rest, d)
    scrs = (scr_a, scr_b)
    for i in range(steps):
        if i % 2 == 0:
            for act in events.pop(i // 2, ()):
                act()
        dots(i, scrs[i % 2])
        if i > 0:
            reduce(i - 1, scrs[(i - 1) % 2])
    reduce(steps - 1, scrs[(steps - 1) % 2])
    for slot in sorted(events):
        for act in events[slot]:
            act()

    owns[1].wait()
    arrived(lat_out.at[: 2 * a], "core")
    for kind, ref in enumerate((key_out, lat_out)):
        every = ref.at[: n - 1]
        remote(every, every, send_sem.at[kind], recv_sem.at[0], ctx=partner).wait_send()


def gather(latents, keys, iq, weights, heads, n):
    rank, rows = latents.shape
    seq = rows * n
    hbm = pl.BlockSpec(memory_space=pl.ANY)
    vmem = pl.BlockSpec(memory_space=pltpu.VMEM)
    m = STEP * heads
    return pl.pallas_call(
        functools.partial(gather_kernel, n, heads),
        out_shape=(
            jax.ShapeDtypeStruct((n, rows, rank), BF16),
            jax.ShapeDtypeStruct((n, rows, keys.shape[1]), BF16),
            jax.ShapeDtypeStruct((rows // 2, seq), F32),
            jax.ShapeDtypeStruct((rows // 2, seq), F32),
        ),
        in_specs=[vmem, vmem, vmem, vmem],
        out_specs=(hbm, vmem, vmem, vmem),
        scratch_shapes=[
            pltpu.VMEM((rows, rank), BF16),
            pltpu.VMEM(weights.shape, F32),
            pltpu.VMEM((m, 4 * rows), F32),
            pltpu.VMEM((m, 4 * rows), F32),
            pltpu.SemaphoreType.DMA((2,)),
            pltpu.SemaphoreType.DMA((7 * (n // 4) - 3,)),
            pltpu.SemaphoreType.DMA((2,)),
        ],
        compiler_params=pltpu.CompilerParams(
            collective_id=0, has_side_effects=True, vmem_limit_bytes=VMEM_LIMIT
        ),
        name="gather",
    )(latents, keys, iq, weights)


def attend_kernel(
    half, n, q_ref, lat_ref, pos_ref, out_ref, low_ref, scr_a, scr_b, top_a, top_b, wide, acc
):
    step = pl.program_id(0)
    seq, depth = lat_ref.shape
    group, _, lanes = q_ref.shape
    count = lanes // 2
    rows = seq // n
    edge = depth // 128 * 128

    @pl.when(step == 0)
    def _():
        lane = lax.broadcasted_iota(jnp.int32, (rows, lanes), 1)
        row = lax.broadcasted_iota(jnp.int32, (rows, lanes), 0)
        own = jnp.where(row <= half * count + lane - (lanes - count), 0.0, NEGATIVE)
        for b in range(n):
            ahead = pos_ref[b] - pos_ref[lax.axis_index("ctx")]
            bias = jnp.where(ahead == 0, own, jnp.where(ahead < 0, 0.0, NEGATIVE))
            at = slice(b * rows, (b + 1) * rows)
            wide[at, :edge] = lat_ref[at, :edge]
            last = lat_ref[at, edge:].astype(F32)
            last = jnp.concatenate([last, jnp.zeros((rows, lanes - last.shape[1]), F32)], axis=1)
            wide[at, edge:] = jnp.where(lane < depth - edge, last, bias).astype(BF16)
        scr_b[...] = jnp.zeros_like(scr_b)
        top_b[...] = jnp.zeros_like(top_b)
        acc[...] = jnp.zeros_like(acc)

    def scores(first, scr, top_ref):
        def part(h):
            return q_ref[h][:, half * count : (half + 1) * count]

        weights = jnp.concatenate([part(first + h) for h in range(4)], axis=1)
        line = lax.broadcasted_iota(jnp.int32, (count, 4 * count), 0)
        column = lax.broadcasted_iota(jnp.int32, (count, 4 * count), 1)
        same = jnp.where(lax.rem(column, count) == line, 1.0, 0.0).astype(BF16)
        weights = jnp.concatenate([weights, same], axis=0)
        piece = seq // PIECES
        top = None
        for r in range(0, seq, piece):
            v = jnp.dot(wide[r : r + piece, :], weights, preferred_element_type=F32)
            scr[r : r + piece, :] = v
            for k in range(0, piece, 8):
                top = v[k : k + 8] if top is None else jnp.maximum(top, v[k : k + 8])
            yield
        top_ref[...] = top

    def softmax(scr, top_ref, use):
        scale = []
        for tile in (slice(0, lanes), slice(lanes, 2 * lanes)):
            top = jnp.max(top_ref[:, tile], axis=0, keepdims=True)
            total = None
            for r in range(0, seq, RUN):
                p = jnp.exp2((scr[r : r + RUN, tile] - top) * (SCALE_ATTN * LOG2E))
                scr[r : r + RUN, tile] = p
                total = p if total is None else total + p
                yield
            total = jnp.sum(total, axis=0, keepdims=True)
            share = 1.0 / (HEADS * total)
            scale.append(share if use is None else jnp.where(use, share, 0.0))
        for r in range(0, seq, RUN):
            acc[r : r + RUN, :] += (
                scr[r : r + RUN, :lanes] * scale[0] + scr[r : r + RUN, lanes:] * scale[1]
            )
            yield

    def together(dots, vectors):
        total = 3 * (seq // RUN)
        done = 0
        for k, _ in enumerate(dots):
            upto = -(-total * WEIGHTS[k] // WEIGHTS[-1])
            while done < upto:
                next(vectors, None)
                done += 1
        for _ in vectors:
            pass

    for k in range(0, group, 8):
        together(scores(k, scr_a, top_a), softmax(scr_b, top_b, step > 0 if k == 0 else None))
        together(scores(k + 4, scr_b, top_b), softmax(scr_a, top_a, None))

    @pl.when(step == pl.num_programs(0) - 1)
    def _():
        for _ in softmax(scr_b, top_b, None):
            pass
        both = jnp.transpose(acc[...])
        out = both[:count] + both[count:]
        out_ref[...] = out
        low_ref[...] = out.astype(BF16)


def attend(q, lat, block_pos, half, n):
    heads, depth, lanes = q.shape
    seq = lat.shape[0]
    count = lanes // 2
    smem = pl.BlockSpec(memory_space=pltpu.SMEM)
    whole = lambda i: (0, 0)
    return pl.pallas_call(
        functools.partial(attend_kernel, half, n),
        grid=(heads // GROUP,),
        out_shape=(
            jax.ShapeDtypeStruct((count, seq), F32),
            jax.ShapeDtypeStruct((count, seq), BF16),
        ),
        in_specs=[
            pl.BlockSpec((GROUP, depth, lanes), lambda i: (i, 0, 0)),
            pl.BlockSpec((seq, depth), whole),
            smem,
        ],
        out_specs=(pl.BlockSpec((count, seq), whole), pl.BlockSpec((count, seq), whole)),
        scratch_shapes=[
            pltpu.VMEM((seq, 2 * lanes), F32),
            pltpu.VMEM((seq, 2 * lanes), F32),
            pltpu.VMEM((8, 2 * lanes), F32),
            pltpu.VMEM((8, 2 * lanes), F32),
            pltpu.VMEM((seq, depth + count), BF16),
            pltpu.VMEM((seq, lanes), F32),
        ],
        compiler_params=pltpu.CompilerParams(vmem_limit_bytes=VMEM_LIMIT),
        cost_estimate=pl.CostEstimate(
            flops=count * heads * seq * depth // 8,
            bytes_accessed=4 * count * heads * depth,
            transcendentals=0,
        ),
        name="attend",
    )(q, lat, block_pos)


def delta_rows(index, target, pos_ref, start, rows):
    count, seq = index.shape
    lane = lax.broadcasted_iota(jnp.int32, (count, rows), 1)
    line = lax.broadcasted_iota(jnp.int32, (count, rows), 0)
    here = pos_ref[lax.axis_index("ctx")] * rows + start + line - lane
    ahead = jnp.concatenate([pos_ref[b] * rows - here for b in range(seq // rows)], axis=1)
    seen = ahead <= 0
    masked = jnp.where(seen, index, NEGATIVE)
    weights = jnp.where(seen, jnp.exp(masked - jnp.max(masked, axis=1, keepdims=True)), 0.0)
    prob = weights * (1.0 / jnp.sum(weights, axis=1, keepdims=True))
    return jnp.where(seen, LOSS_SCALE * (prob - target), 0.0).astype(BF16).astype(F32)


def back_kernel(
    heads, rows, iq_ref, w_ref, key_ref, pos_ref, peers_i, own_i, own_t, peers_t,
    gq_ref, gk_ref, scr, coef, dscr, w_scaled,
):
    step = pl.program_id(0)
    start = step * TOK
    w_scaled[...] = pltpu.roll(w_ref[...], rows - start, 1) * key_ref.shape[1] ** (-0.5)

    @pl.when(step == 0)
    def _():
        gk_ref[...] = jnp.zeros_like(gk_ref)

    scr[...] = dot_t(iq_ref[...], key_ref[...])
    index, target = own_i[...], own_t[...]
    for k in range(peers_i.shape[0]):
        index = index + peers_i[k]
        target = target + peers_t[k].astype(F32)
    dscr[...] = delta_rows(index, target, pos_ref, start, rows)
    for t in range(TOK):
        for g in range(0, heads, 8):
            r = t * heads + g
            wide = jnp.broadcast_to(w_scaled[g : g + 8, t : t + 1], (8, dscr.shape[1]))
            value = dscr[t : t + 1, :] * wide
            coef[r : r + 8, :] = jnp.where(scr[r : r + 8, :] > 0.0, value, 0.0).astype(BF16)
    gq_ref[...] = jnp.dot(coef[...], key_ref[...], preferred_element_type=F32)
    gk_ref[...] += lax.dot_general(
        iq_ref[...], coef[...], (((0,), (0,)), ((), ())), preferred_element_type=F32
    )


def back(iq, weights, keys, block_pos, peers_i, own_i, own_t, peers_t, heads):
    depth = iq.shape[1]
    rows = weights.shape[1]
    count, seq = own_t.shape
    m = TOK * heads
    others = peers_i.shape[0]
    return pl.pallas_call(
        functools.partial(back_kernel, heads, rows),
        grid=(count // TOK,),
        out_shape=(
            jax.ShapeDtypeStruct(iq.shape, F32),
            jax.ShapeDtypeStruct((depth, seq), F32),
        ),
        in_specs=[
            pl.BlockSpec((m, depth), lambda i: (i, 0)),
            pl.BlockSpec(weights.shape, lambda i: (0, 0)),
            pl.BlockSpec((seq, depth), lambda i: (0, 0)),
            pl.BlockSpec(memory_space=pltpu.SMEM),
            pl.BlockSpec((others, TOK, seq), lambda i: (0, i, 0)),
            pl.BlockSpec((TOK, seq), lambda i: (i, 0)),
            pl.BlockSpec((TOK, seq), lambda i: (i, 0)),
            pl.BlockSpec((others, TOK, seq), lambda i: (0, i, 0)),
        ],
        out_specs=(
            pl.BlockSpec((m, depth), lambda i: (i, 0)),
            pl.BlockSpec((depth, seq), lambda i: (0, 0)),
        ),
        scratch_shapes=[
            pltpu.VMEM((m, seq), F32),
            pltpu.VMEM((m, seq), BF16),
            pltpu.VMEM((TOK, seq), F32),
            pltpu.VMEM(weights.shape, F32),
        ],
        compiler_params=pltpu.CompilerParams(vmem_limit_bytes=VMEM_LIMIT),
        cost_estimate=pl.CostEstimate(
            flops=8 * count * heads * seq * depth,
            bytes_accessed=8 * count * heads * depth,
            transcendentals=0,
        ),
        name="back",
    )(iq, weights, keys, block_pos, peers_i, own_i, own_t, peers_t)


def finish_kernel(
    n, heads, ranks, iq_ref, w_ref, key_ref, pos_ref, peers_i, own_i, own_t, peers_t, carried,
    gq_ref, put4, got4, scr, coef, dscr, w_scaled, acc,
    sum0, put1, got1, sum1, put2, got2, put3, got3, ssem, rsem,
):
    z, x, c, a = place(n)
    y = lax.axis_index("head")
    barrier = pltpu.get_barrier_semaphore()
    greeted = [dict(ctx=at(z, 1 - x, c)), dict(ctx=at(z, x, 1 - c))]
    greeted += [dict(ctx=at(lax.rem(z + d, a), x, c)) for d in range(1, a)]
    greeted += [dict(head=lax.rem(y + d, ranks)) for d in range(1, ranks)]
    for where in greeted:
        pl.semaphore_signal(barrier, inc=1, device_id=where, device_id_type=MESH)

    depth = key_ref.shape[1]
    count, seq = own_t.shape
    rows = w_ref.shape[1]
    width = 4 * rows
    m = TOK * heads
    w_scaled[...] = w_ref[...] * depth ** (-0.5)
    for t in range(0, count, TOK):
        span = slice(t, t + TOK)
        index, target = own_i[span, :], own_t[span, :]
        for k in range(ranks - 1):
            index = index + peers_i[k, span, :]
            target = target + peers_t[k, span, :].astype(F32)
        dscr[span, :] = delta_rows(index, target, pos_ref, rows - count + t, rows)

    order = [*range(1, a), 0]

    def copy(stage, e, src, dst, **where):
        k = stage * a + e
        return remote(src, dst, ssem.at[k], rsem.at[k], **where)

    def core(e):
        return copy(0, e, put1.at[e], got1.at[e], ctx=at(z, x, 1 - c))

    def side(e):
        return copy(1, e, put2.at[e], got2.at[e], ctx=at(z, 1 - x, c))

    def line(e):
        to = lax.rem(z + order[e], a)
        return copy(2, e, put3.at[e], got3.at[e], ctx=at(to, x, c))

    def compute(e):
        zd = lax.rem(z + order[e], a)
        cols = pl.ds(pl.multiple_of(zd * width, width), width)
        held = key_ref[cols, :]
        acc[...] = carried[:, cols]
        for t in range(0, count, TOK):
            part = slice(t * heads, t * heads + m)
            iq = iq_ref[part, :]
            scr[...] = dot_t(iq, held)
            for u in range(TOK):
                row = dscr[t + u : t + u + 1, cols]
                tok = rows - count + t + u
                for g in range(0, heads, 8):
                    r = u * heads + g
                    wide = jnp.broadcast_to(w_scaled[g : g + 8, tok : tok + 1], (8, width))
                    coef[r : r + 8, :] = jnp.where(
                        scr[r : r + 8, :] > 0.0, row * wide, 0.0
                    ).astype(BF16)
            grad = jnp.dot(coef[...], held, preferred_element_type=F32)
            gq_ref[part, :] = grad if e == 0 else gq_ref[part, :] + grad
            acc[...] += lax.dot_general(
                iq, coef[...], (((0,), (0,)), ((), ())), preferred_element_type=F32
            )
        sum0[e] = jnp.transpose(acc[...]).reshape(2, 2, rows, depth)

    def first(e):
        put1[e] = sum0[e, :, 1 - c].astype(BF16)
        core(e).start()

    def second(e):
        core(e).wait_recv()
        sum1[e] = sum0[e, x, c] + got1[e, x].astype(F32)
        put2[e] = (sum0[e, 1 - x, c] + got1[e, 1 - x].astype(F32)).astype(BF16)
        side(e).start()

    def third(e):
        side(e).wait_recv()
        total = sum1[e] + got2[e].astype(F32)
        if e < a - 1:
            put3[e] = total.astype(BF16)
            line(e).start()
        else:
            for k in range(a - 1):
                line(k).wait_recv()
                total = total + got3[k].astype(F32)
            put4[...] = total

    for e in range(a):
        compute(e)
        if e == 0:
            pl.semaphore_wait(barrier, len(greeted))
        first(e)
        if e > 0:
            second(e - 1)
        if e > 1:
            third(e - 2)
    second(a - 1)
    third(a - 2)
    third(a - 1)
    last = []
    for d in range(1, ranks):
        item = remote(
            put4, got4.at[d - 1], ssem.at[3 * a + d - 1], rsem.at[3 * a + d - 1],
            head=lax.rem(y + d, ranks),
        )
        item.start()
        last.append(item)
    for e in range(a):
        core(e).wait_send()
        side(e).wait_send()
        if e < a - 1:
            line(e).wait_send()
    for item in last:
        item.wait()


def finish(iq, weights, keys, block_pos, peers_i, own_i, own_t, peers_t, carried, heads, n, ranks):
    depth = iq.shape[1]
    rows = weights.shape[1]
    count, seq = own_t.shape
    half = count * heads
    m = TOK * heads
    a = n // 4
    vmem = pl.BlockSpec(memory_space=pltpu.VMEM)
    grad, own, peers = pl.pallas_call(
        functools.partial(finish_kernel, n, heads, ranks),
        grid=(1,),
        out_shape=(
            jax.ShapeDtypeStruct((half, depth), F32),
            jax.ShapeDtypeStruct((rows, depth), F32),
            jax.ShapeDtypeStruct((ranks - 1, rows, depth), F32),
        ),
        in_specs=[
            pl.BlockSpec((half, depth), lambda i: (1, 0)),
            vmem, vmem, pl.BlockSpec(memory_space=pltpu.SMEM), vmem, vmem, vmem, vmem, vmem,
        ],
        out_specs=(vmem, vmem, vmem),
        scratch_shapes=[
            pltpu.VMEM((m, 4 * rows), F32),
            pltpu.VMEM((m, 4 * rows), BF16),
            pltpu.VMEM((count, seq), F32),
            pltpu.VMEM(weights.shape, F32),
            pltpu.VMEM((depth, 4 * rows), F32),
            pltpu.VMEM((a, 2, 2, rows, depth), F32),
            pltpu.VMEM((a, 2, rows, depth), BF16),
            pltpu.VMEM((a, 2, rows, depth), BF16),
            pltpu.VMEM((a, rows, depth), F32),
            pltpu.VMEM((a, rows, depth), BF16),
            pltpu.VMEM((a, rows, depth), BF16),
            pltpu.VMEM((a, rows, depth), BF16),
            pltpu.VMEM((a, rows, depth), BF16),
            pltpu.SemaphoreType.DMA((3 * a + ranks - 1,)),
            pltpu.SemaphoreType.DMA((3 * a + ranks - 1,)),
        ],
        compiler_params=pltpu.CompilerParams(
            collective_id=1, has_side_effects=True, vmem_limit_bytes=VMEM_LIMIT
        ),
        name="finish",
    )(iq, weights, keys, block_pos, peers_i, own_i, own_t, peers_t, carried)
    return grad, own + jnp.sum(peers, axis=0)


def swap(value, ranks):
    return jnp.stack(
        [
            lax.ppermute(value, "head", [(i, (i + d) % ranks) for i in range(ranks)])
            for d in range(1, ranks)
        ]
    )


def body(queries, latents, index_queries, index_keys, head_weights, block_pos):
    rows, heads, rank = queries.shape
    depth = index_queries.shape[2]
    n, ranks = lax.axis_size("ctx"), lax.axis_size("head")
    seq = rows * n
    q = jnp.transpose(queries, (1, 2, 0))
    iq = index_queries.reshape(rows * heads, depth)
    weights = jnp.transpose(head_weights)

    lat, keys, *own_i = gather(jnp.transpose(latents), index_keys, iq, weights, heads, n)
    lat = lat.reshape(seq, rank)
    keys = keys.reshape(seq, depth)
    peers_i = [swap(value, ranks) for value in own_i]
    own_t, peers_t = [], []
    for k in range(2):
        full, low = attend(q, lat, block_pos, k, n)
        own_t.append(full)
        peers_t.append(swap(low, ranks))
    first, carried = back(
        iq, weights, keys, block_pos, peers_i[0], own_i[0], own_t[0], peers_t[0], heads
    )
    second, grad_keys = finish(
        iq, weights, keys, block_pos, peers_i[1], own_i[1], own_t[1], peers_t[1], carried, heads,
        n, ranks,
    )
    grad = lax.dynamic_update_slice(first, second, (second.shape[0], 0))
    return grad.reshape(rows, heads, depth), grad_keys


def solution(mesh):
    return jax.shard_map(
        body,
        mesh=mesh,
        in_specs=(
            P("ctx", "head", None),
            P("ctx", None),
            P("ctx", "head", None),
            P("ctx", None),
            P("ctx", "head"),
            P(),
        ),
        out_specs=(P("ctx", "head", None), P("ctx", None)),
        check_vma=False,
    )
```

```python
import functools
import math

import jax
import jax.numpy as jnp
from jax import lax
from jax.experimental import pallas as pl
from jax.experimental.pallas import tpu as pltpu
from jax.sharding import PartitionSpec as P

HEADS = 64
SCALE_ATTN = 192.0 ** (-0.5)
LOSS_SCALE = 1024.0
NEGATIVE = -1e30
LOG2E = math.log2(math.e)
MESH = pl.DeviceIdType.MESH
F32 = jnp.float32
BF16 = jnp.bfloat16
TOK = 16
STEP = 16
LAG = 1
PIECES = 2
RUN = 64
GROUP = 8
WEIGHTS = (1, 3, 4)
VMEM_LIMIT = 60 * 1024 * 1024


def place(n):
    me = lax.axis_index("ctx")
    a = n // 4
    return me // 4, (me // 2) % 2, me % 2, a


def at(z, x, c):
    return (z * 2 + x) * 2 + c


def remote(src, dst, send, recv, **where):
    return pltpu.make_async_remote_copy(
        src_ref=src, dst_ref=dst, send_sem=send, recv_sem=recv, device_id=where, device_id_type=MESH
    )


def dot_t(a, b):
    return lax.dot_general(a, b, (((1,), (1,)), ((), ())), preferred_element_type=F32)


def gather_kernel(
    n, heads, lat_ref, key_ref, iq_ref, w_ref, lat_out, key_out, idx_first, idx_second,
    lat_own, w_scaled, scr_a, scr_b, send_sem, recv_sem, own_sem,
):
    z, x, c, a = place(n)
    y = lax.axis_index("head")
    other_y = y + 1 - 2 * (y % 2)
    partner = at(z, x, 1 - c)
    rows, depth = key_ref.shape
    part = rows // 2
    mine, others = 1 + y % 2, 2 - y % 2
    me = at(z, x, c)
    barrier = pltpu.get_barrier_semaphore()
    greeted = [dict(ctx=at(z, 1 - x, c)), dict(ctx=partner), dict(head=other_y)]
    greeted += [dict(ctx=at(lax.rem(z + d, a), x, c)) for d in range(1, a)]
    for where in greeted:
        pl.semaphore_signal(barrier, inc=1, device_id=where, device_id_type=MESH)
    rank = lat_ref.shape[0]
    for r in range(0, rank, 128):
        end = min(r + 128, rank)
        lat_own[:, r:end] = jnp.transpose(lat_ref[r:end, :].astype(F32)).astype(BF16)
    owns = []
    for k, (src, dst) in enumerate(((key_ref, key_out), (lat_own, lat_out))):
        own = pltpu.make_async_copy(src, dst.at[me], own_sem.at[k])
        own.start()
        owns.append(own)
    w_scaled[...] = w_ref[...] * depth ** (-0.5)
    pl.semaphore_wait(barrier, len(greeted))

    above = a - 1
    spots = dict(
        key_near=0, key_column=0, key_crossed=above, key_core=2 * above + 1,
        near=3 * a - 1, column=3 * a - 1, crossed=3 * a - 1 + above,
        column_rest=3 * a - 1 + 2 * above, crossed_rest=3 * a - 1 + 3 * above,
        core=3 * a + 4 * above,
    )

    def half(ref, k):
        return ref.at[pl.ds(pl.multiple_of((k - 1) * part, part), part)]

    def send(k, slot, spot, d, **where):
        first = slot is me
        if isinstance(k, int) and k == 0:
            src, dst, kind = (key_ref if first else key_out.at[slot]), key_out.at[slot], 0
        else:
            dst, kind = half(lat_out.at[slot], k), 1
            src = half(lat_own, k) if first else dst
        remote(src, dst, send_sem.at[kind], recv_sem.at[spots[spot] + d], **where).start()

    def to_core(k, slot, d):
        if isinstance(k, int) and k == 0:
            send(k, slot, "key_core", d, ctx=partner)
        else:
            send(k, slot, "core", 0, ctx=partner)

    def to_x(k, slot, spot, d=0):
        send(k, slot, spot, d, ctx=at(z, 1 - x, c))

    def to_y(k, slot, spot, d):
        send(k, slot, spot, d, head=other_y)

    def to_z(k, spot):
        for d in range(1, a):
            send(k, me, spot, d, ctx=at(lax.rem(z + d, a), x, c))

    def arrived(dst, spot, d=0):
        remote(dst, dst, send_sem.at[0], recv_sem.at[spots[spot] + d], ctx=partner).wait_recv()

    def level(d):
        return lax.rem(z + a - d, a)

    def key_near():
        slot = at(z, 1 - x, c)
        arrived(key_out.at[slot], "key_near")
        to_core(0, slot, 0)
        owns[0].wait()
        key_ready(0)

    def key_ready(d):
        arrived(key_out.at[pl.ds(level(d) * 4, 2)], "key_core", d)

    def key_column(d):
        slot = at(level(d), x, c)
        arrived(key_out.at[slot], "key_column", d)
        to_x(0, slot, "key_crossed", d)
        to_core(0, slot, d)

    def key_crossed(d):
        slot = at(level(d), 1 - x, c)
        arrived(key_out.at[slot], "key_crossed", d)
        to_core(0, slot, d)

    def near():
        slot = at(z, 1 - x, c)
        arrived(lat_out.at[slot], "near")
        for k in (mine, others):
            to_core(k, slot, 0)

    def column(d):
        slot = at(level(d), x, c)
        arrived(half(lat_out.at[slot], mine), "column", d)
        to_x(mine, slot, "crossed", d)
        to_y(mine, slot, "column_rest", d)
        to_core(mine, slot, d)

    def crossed(d):
        slot = at(level(d), 1 - x, c)
        arrived(half(lat_out.at[slot], mine), "crossed", d)
        to_y(mine, slot, "crossed_rest", d)
        to_core(mine, slot, d)

    def column_rest(d):
        slot = at(level(d), x, c)
        arrived(half(lat_out.at[slot], others), "column_rest", d)
        to_core(others, slot, d)

    def crossed_rest(d):
        slot = at(level(d), 1 - x, c)
        arrived(half(lat_out.at[slot], others), "crossed_rest", d)
        to_core(others, slot, d)

    to_z(0, "key_column")
    to_x(0, me, "key_near")
    to_core(0, me, 0)
    to_z(mine, "column")
    to_x(mine, me, "near")
    to_x(others, me, "near")
    to_core(mine, me, 0)
    to_core(others, me, 0)

    width = 4 * rows
    m = scr_a.shape[0]
    chunks = iq_ref.shape[0] // m
    steps = chunks * a

    def dots(i, scr):
        r = i % chunks * m
        held = key_out[pl.ds(level(i // chunks) * 4, 4)].reshape(width, depth)
        for h in range(0, m, m // 2):
            scr[h : h + m // 2, :] = dot_t(iq_ref[r + h : r + h + m // 2, :], held)

    def reduce(i, scr):
        first = i % chunks * m
        place_out = pl.ds(pl.multiple_of(level(i // chunks) * width, width), width)
        for t in range(0, m // heads, 8):
            sums = []
            for u in range(t, t + 8):
                total = None
                for g in range(0, heads, 8):
                    r = u * heads + g
                    tok = first // heads + u
                    w = jnp.broadcast_to(w_scaled[g : g + 8, tok : tok + 1], (8, width))
                    term = jnp.maximum(scr[r : r + 8, :], 0.0) * w
                    total = term if total is None else total + term
                sums.append(jnp.sum(total, axis=0, keepdims=True))
            row = first // heads + t
            idx_ref, row = (idx_first, row) if row < part else (idx_second, row - part)
            idx_ref[row : row + 8, place_out] = jnp.concatenate(sums, axis=0)

    events = {}

    def plan(slot, act, *args):
        events.setdefault(slot, []).append(functools.partial(act, *args))

    plan(0, key_near)
    for d in range(1, a):
        plan(1, key_column, d)
    plan(1, near)
    for d in range(1, a):
        plan(1 + d, column, d)
    for d in range(1, a):
        plan(4, key_crossed, d)
        plan(d * chunks // 2, key_ready, d)
        plan(3 + 2 * d, crossed, d)
        plan(4 + 2 * d, column_rest, d)
        plan(6 + 2 * d, crossed_rest, d)
    scrs = (scr_a, scr_b)
    for i in range(steps):
        if i % 2 == 0:
            for act in events.pop(i // 2, ()):
                act()
        dots(i, scrs[i % 2])
        if i > 0:
            reduce(i - 1, scrs[(i - 1) % 2])
    reduce(steps - 1, scrs[(steps - 1) % 2])
    for slot in sorted(events):
        for act in events[slot]:
            act()

    owns[1].wait()
    arrived(lat_out.at[: 2 * a], "core")
    for kind, ref in enumerate((key_out, lat_out)):
        every = ref.at[: n - 1]
        remote(every, every, send_sem.at[kind], recv_sem.at[0], ctx=partner).wait_send()


def gather(latents, keys, iq, weights, heads, n):
    rank, rows = latents.shape
    seq = rows * n
    hbm = pl.BlockSpec(memory_space=pl.ANY)
    vmem = pl.BlockSpec(memory_space=pltpu.VMEM)
    m = STEP * heads
    return pl.pallas_call(
        functools.partial(gather_kernel, n, heads),
        out_shape=(
            jax.ShapeDtypeStruct((n, rows, rank), BF16),
            jax.ShapeDtypeStruct((n, rows, keys.shape[1]), BF16),
            jax.ShapeDtypeStruct((rows // 2, seq), F32),
            jax.ShapeDtypeStruct((rows // 2, seq), F32),
        ),
        in_specs=[vmem, vmem, vmem, vmem],
        out_specs=(hbm, vmem, vmem, vmem),
        scratch_shapes=[
            pltpu.VMEM((rows, rank), BF16),
            pltpu.VMEM(weights.shape, F32),
            pltpu.VMEM((m, 4 * rows), F32),
            pltpu.VMEM((m, 4 * rows), F32),
            pltpu.SemaphoreType.DMA((2,)),
            pltpu.SemaphoreType.DMA((7 * (n // 4) - 3,)),
            pltpu.SemaphoreType.DMA((2,)),
        ],
        compiler_params=pltpu.CompilerParams(
            collective_id=0, has_side_effects=True, vmem_limit_bytes=VMEM_LIMIT
        ),
        name="gather",
    )(latents, keys, iq, weights)


def attend_kernel(
    half, n, q_ref, lat_ref, pos_ref, out_ref, low_ref, scr_a, scr_b, top_a, top_b, wide, acc
):
    step = pl.program_id(0)
    seq, depth = lat_ref.shape
    group, _, lanes = q_ref.shape
    count = lanes // 2
    rows = seq // n
    edge = depth // 128 * 128

    @pl.when(step == 0)
    def _():
        lane = lax.broadcasted_iota(jnp.int32, (rows, lanes), 1)
        row = lax.broadcasted_iota(jnp.int32, (rows, lanes), 0)
        own = jnp.where(row <= half * count + lane - (lanes - count), 0.0, NEGATIVE)
        for b in range(n):
            ahead = pos_ref[b] - pos_ref[lax.axis_index("ctx")]
            bias = jnp.where(ahead == 0, own, jnp.where(ahead < 0, 0.0, NEGATIVE))
            at = slice(b * rows, (b + 1) * rows)
            wide[at, :edge] = lat_ref[at, :edge]
            last = lat_ref[at, edge:].astype(F32)
            last = jnp.concatenate([last, jnp.zeros((rows, lanes - last.shape[1]), F32)], axis=1)
            wide[at, edge:] = jnp.where(lane < depth - edge, last, bias).astype(BF16)
        scr_b[...] = jnp.zeros_like(scr_b)
        top_b[...] = jnp.zeros_like(top_b)
        acc[...] = jnp.zeros_like(acc)

    def scores(first, scr, top_ref):
        def part(h):
            return q_ref[h][:, half * count : (half + 1) * count]

        weights = jnp.concatenate([part(first + h) for h in range(4)], axis=1)
        line = lax.broadcasted_iota(jnp.int32, (count, 4 * count), 0)
        column = lax.broadcasted_iota(jnp.int32, (count, 4 * count), 1)
        same = jnp.where(lax.rem(column, count) == line, 1.0, 0.0).astype(BF16)
        weights = jnp.concatenate([weights, same], axis=0)
        piece = seq // PIECES
        top = None
        for r in range(0, seq, piece):
            v = jnp.dot(wide[r : r + piece, :], weights, preferred_element_type=F32)
            scr[r : r + piece, :] = v
            for k in range(0, piece, 8):
                top = v[k : k + 8] if top is None else jnp.maximum(top, v[k : k + 8])
            yield
        top_ref[...] = top

    def softmax(scr, top_ref, use):
        scale = []
        for tile in (slice(0, lanes), slice(lanes, 2 * lanes)):
            top = jnp.max(top_ref[:, tile], axis=0, keepdims=True)
            total = None
            for r in range(0, seq, RUN):
                p = jnp.exp2((scr[r : r + RUN, tile] - top) * (SCALE_ATTN * LOG2E))
                scr[r : r + RUN, tile] = p
                total = p if total is None else total + p
                yield
            total = jnp.sum(total, axis=0, keepdims=True)
            share = 1.0 / (HEADS * total)
            scale.append(share if use is None else jnp.where(use, share, 0.0))
        for r in range(0, seq, RUN):
            acc[r : r + RUN, :] += (
                scr[r : r + RUN, :lanes] * scale[0] + scr[r : r + RUN, lanes:] * scale[1]
            )
            yield

    def together(dots, vectors):
        total = 3 * (seq // RUN)
        done = 0
        for k, _ in enumerate(dots):
            upto = -(-total * WEIGHTS[k] // WEIGHTS[-1])
            while done < upto:
                next(vectors, None)
                done += 1
        for _ in vectors:
            pass

    for k in range(0, group, 8):
        together(scores(k, scr_a, top_a), softmax(scr_b, top_b, step > 0 if k == 0 else None))
        together(scores(k + 4, scr_b, top_b), softmax(scr_a, top_a, None))

    @pl.when(step == pl.num_programs(0) - 1)
    def _():
        for _ in softmax(scr_b, top_b, None):
            pass
        both = jnp.transpose(acc[...])
        out = both[:count] + both[count:]
        out_ref[...] = out
        low_ref[...] = out.astype(BF16)


def attend(q, lat, block_pos, half, n):
    heads, depth, lanes = q.shape
    seq = lat.shape[0]
    count = lanes // 2
    smem = pl.BlockSpec(memory_space=pltpu.SMEM)
    whole = lambda i: (0, 0)
    return pl.pallas_call(
        functools.partial(attend_kernel, half, n),
        grid=(heads // GROUP,),
        out_shape=(
            jax.ShapeDtypeStruct((count, seq), F32),
            jax.ShapeDtypeStruct((count, seq), BF16),
        ),
        in_specs=[
            pl.BlockSpec((GROUP, depth, lanes), lambda i: (i, 0, 0)),
            pl.BlockSpec((seq, depth), whole),
            smem,
        ],
        out_specs=(pl.BlockSpec((count, seq), whole), pl.BlockSpec((count, seq), whole)),
        scratch_shapes=[
            pltpu.VMEM((seq, 2 * lanes), F32),
            pltpu.VMEM((seq, 2 * lanes), F32),
            pltpu.VMEM((8, 2 * lanes), F32),
            pltpu.VMEM((8, 2 * lanes), F32),
            pltpu.VMEM((seq, depth + count), BF16),
            pltpu.VMEM((seq, lanes), F32),
        ],
        compiler_params=pltpu.CompilerParams(vmem_limit_bytes=VMEM_LIMIT),
        cost_estimate=pl.CostEstimate(
            flops=count * heads * seq * depth // 8,
            bytes_accessed=4 * count * heads * depth,
            transcendentals=0,
        ),
        name="attend",
    )(q, lat, block_pos)


def delta_rows(index, target, pos_ref, start, rows):
    count, seq = index.shape
    lane = lax.broadcasted_iota(jnp.int32, (count, rows), 1)
    line = lax.broadcasted_iota(jnp.int32, (count, rows), 0)
    here = pos_ref[lax.axis_index("ctx")] * rows + start + line - lane
    ahead = jnp.concatenate([pos_ref[b] * rows - here for b in range(seq // rows)], axis=1)
    seen = ahead <= 0
    masked = jnp.where(seen, index, NEGATIVE)
    weights = jnp.where(seen, jnp.exp(masked - jnp.max(masked, axis=1, keepdims=True)), 0.0)
    prob = weights * (1.0 / jnp.sum(weights, axis=1, keepdims=True))
    return jnp.where(seen, LOSS_SCALE * (prob - target), 0.0).astype(BF16).astype(F32)


def back_kernel(
    heads, rows, iq_ref, w_ref, key_ref, pos_ref, peers_i, own_i, own_t, peers_t,
    gq_ref, gk_ref, scr, coef, dscr, w_scaled,
):
    step = pl.program_id(0)
    start = step * TOK
    w_scaled[...] = pltpu.roll(w_ref[...], rows - start, 1) * key_ref.shape[1] ** (-0.5)

    @pl.when(step == 0)
    def _():
        gk_ref[...] = jnp.zeros_like(gk_ref)

    scr[...] = dot_t(iq_ref[...], key_ref[...])
    index, target = own_i[...], own_t[...]
    for k in range(peers_i.shape[0]):
        index = index + peers_i[k]
        target = target + peers_t[k].astype(F32)
    dscr[...] = delta_rows(index, target, pos_ref, start, rows)
    for t in range(TOK):
        for g in range(0, heads, 8):
            r = t * heads + g
            wide = jnp.broadcast_to(w_scaled[g : g + 8, t : t + 1], (8, dscr.shape[1]))
            value = dscr[t : t + 1, :] * wide
            coef[r : r + 8, :] = jnp.where(scr[r : r + 8, :] > 0.0, value, 0.0).astype(BF16)
    gq_ref[...] = jnp.dot(coef[...], key_ref[...], preferred_element_type=F32)
    gk_ref[...] += lax.dot_general(
        iq_ref[...], coef[...], (((0,), (0,)), ((), ())), preferred_element_type=F32
    )


def back(iq, weights, keys, block_pos, peers_i, own_i, own_t, peers_t, heads):
    depth = iq.shape[1]
    rows = weights.shape[1]
    count, seq = own_t.shape
    m = TOK * heads
    others = peers_i.shape[0]
    return pl.pallas_call(
        functools.partial(back_kernel, heads, rows),
        grid=(count // TOK,),
        out_shape=(
            jax.ShapeDtypeStruct(iq.shape, F32),
            jax.ShapeDtypeStruct((depth, seq), F32),
        ),
        in_specs=[
            pl.BlockSpec((m, depth), lambda i: (i, 0)),
            pl.BlockSpec(weights.shape, lambda i: (0, 0)),
            pl.BlockSpec((seq, depth), lambda i: (0, 0)),
            pl.BlockSpec(memory_space=pltpu.SMEM),
            pl.BlockSpec((others, TOK, seq), lambda i: (0, i, 0)),
            pl.BlockSpec((TOK, seq), lambda i: (i, 0)),
            pl.BlockSpec((TOK, seq), lambda i: (i, 0)),
            pl.BlockSpec((others, TOK, seq), lambda i: (0, i, 0)),
        ],
        out_specs=(
            pl.BlockSpec((m, depth), lambda i: (i, 0)),
            pl.BlockSpec((depth, seq), lambda i: (0, 0)),
        ),
        scratch_shapes=[
            pltpu.VMEM((m, seq), F32),
            pltpu.VMEM((m, seq), BF16),
            pltpu.VMEM((TOK, seq), F32),
            pltpu.VMEM(weights.shape, F32),
        ],
        compiler_params=pltpu.CompilerParams(vmem_limit_bytes=VMEM_LIMIT),
        cost_estimate=pl.CostEstimate(
            flops=8 * count * heads * seq * depth,
            bytes_accessed=8 * count * heads * depth,
            transcendentals=0,
        ),
        name="back",
    )(iq, weights, keys, block_pos, peers_i, own_i, own_t, peers_t)


def finish_kernel(
    n, heads, ranks, iq_ref, w_ref, key_ref, pos_ref, peers_i, own_i, own_t, peers_t, carried,
    gq_ref, out_ref, got4, put4, scr, coef, dscr, w_scaled, acc,
    sum0, put1, got1, sum1, put2, got2, put3, got3, ssem, rsem,
):
    z, x, c, a = place(n)
    y = lax.axis_index("head")
    barrier = pltpu.get_barrier_semaphore()
    greeted = [dict(ctx=at(z, 1 - x, c)), dict(ctx=at(z, x, 1 - c))]
    greeted += [dict(ctx=at(lax.rem(z + d, a), x, c)) for d in range(1, a)]
    greeted += [dict(head=lax.rem(y + d, ranks)) for d in range(1, ranks)]
    for where in greeted:
        pl.semaphore_signal(barrier, inc=1, device_id=where, device_id_type=MESH)

    depth = key_ref.shape[1]
    count, seq = own_t.shape
    rows = w_ref.shape[1]
    width = 4 * rows
    m = TOK * heads
    w_scaled[...] = w_ref[...] * depth ** (-0.5)
    for t in range(0, count, TOK):
        span = slice(t, t + TOK)
        index, target = own_i[span, :], own_t[span, :]
        for k in range(ranks - 1):
            index = index + peers_i[k, span, :]
            target = target + peers_t[k, span, :].astype(F32)
        dscr[span, :] = delta_rows(index, target, pos_ref, rows - count + t, rows)

    order = [*range(1, a), 0]

    def copy(stage, e, src, dst, **where):
        k = stage * a + e
        return remote(src, dst, ssem.at[k], rsem.at[k], **where)

    def core(e):
        return copy(0, e, put1.at[e], got1.at[e], ctx=at(z, x, 1 - c))

    def side(e):
        return copy(1, e, put2.at[e], got2.at[e], ctx=at(z, 1 - x, c))

    def line(e):
        to = lax.rem(z + order[e], a)
        return copy(2, e, put3.at[e], got3.at[e], ctx=at(to, x, c))

    def compute(e):
        zd = lax.rem(z + order[e], a)
        cols = pl.ds(pl.multiple_of(zd * width, width), width)
        held = key_ref[cols, :]
        acc[...] = carried[:, cols]
        for t in range(0, count, TOK):
            part = slice(t * heads, t * heads + m)
            iq = iq_ref[part, :]
            scr[...] = dot_t(iq, held)
            for u in range(TOK):
                row = dscr[t + u : t + u + 1, cols]
                tok = rows - count + t + u
                for g in range(0, heads, 8):
                    r = u * heads + g
                    wide = jnp.broadcast_to(w_scaled[g : g + 8, tok : tok + 1], (8, width))
                    coef[r : r + 8, :] = jnp.where(
                        scr[r : r + 8, :] > 0.0, row * wide, 0.0
                    ).astype(BF16)
            grad = jnp.dot(coef[...], held, preferred_element_type=F32)
            gq_ref[part, :] = grad if e == 0 else gq_ref[part, :] + grad
            acc[...] += lax.dot_general(
                iq, coef[...], (((0,), (0,)), ((), ())), preferred_element_type=F32
            )
        sum0[e] = jnp.transpose(acc[...]).reshape(2, 2, rows, depth)

    def first(e):
        put1[e] = sum0[e, :, 1 - c].astype(BF16)
        core(e).start()

    def second(e):
        core(e).wait_recv()
        sum1[e] = sum0[e, x, c] + got1[e, x].astype(F32)
        put2[e] = (sum0[e, 1 - x, c] + got1[e, 1 - x].astype(F32)).astype(BF16)
        side(e).start()

    def third(e):
        side(e).wait_recv()
        total = sum1[e] + got2[e].astype(F32)
        if e < a - 1:
            put3[e] = total.astype(BF16)
            line(e).start()
        else:
            for k in range(a - 1):
                line(k).wait_recv()
                total = total + got3[k].astype(F32)
            out_ref[...] = total
            put4[...] = total.astype(BF16)

    for e in range(a):
        compute(e)
        if e == 0:
            pl.semaphore_wait(barrier, len(greeted))
        first(e)
        if e > 0:
            second(e - 1)
        if e > 1:
            third(e - 2)
    second(a - 1)
    third(a - 2)
    third(a - 1)
    last = []
    for d in range(1, ranks):
        item = remote(
            put4, got4.at[d - 1], ssem.at[3 * a + d - 1], rsem.at[3 * a + d - 1],
            head=lax.rem(y + d, ranks),
        )
        item.start()
        last.append(item)
    for e in range(a):
        core(e).wait_send()
        side(e).wait_send()
        if e < a - 1:
            line(e).wait_send()
    for item in last:
        item.wait()


def finish(iq, weights, keys, block_pos, peers_i, own_i, own_t, peers_t, carried, heads, n, ranks):
    depth = iq.shape[1]
    rows = weights.shape[1]
    count, seq = own_t.shape
    half = count * heads
    m = TOK * heads
    a = n // 4
    vmem = pl.BlockSpec(memory_space=pltpu.VMEM)
    grad, own, peers = pl.pallas_call(
        functools.partial(finish_kernel, n, heads, ranks),
        grid=(1,),
        out_shape=(
            jax.ShapeDtypeStruct((half, depth), F32),
            jax.ShapeDtypeStruct((rows, depth), F32),
            jax.ShapeDtypeStruct((ranks - 1, rows, depth), BF16),
        ),
        in_specs=[
            pl.BlockSpec((half, depth), lambda i: (1, 0)),
            vmem, vmem, pl.BlockSpec(memory_space=pltpu.SMEM), vmem, vmem, vmem, vmem, vmem,
        ],
        out_specs=(vmem, vmem, vmem),
        scratch_shapes=[
            pltpu.VMEM((rows, depth), BF16),
            pltpu.VMEM((m, 4 * rows), F32),
            pltpu.VMEM((m, 4 * rows), BF16),
            pltpu.VMEM((count, seq), F32),
            pltpu.VMEM(weights.shape, F32),
            pltpu.VMEM((depth, 4 * rows), F32),
            pltpu.VMEM((a, 2, 2, rows, depth), F32),
            pltpu.VMEM((a, 2, rows, depth), BF16),
            pltpu.VMEM((a, 2, rows, depth), BF16),
            pltpu.VMEM((a, rows, depth), F32),
            pltpu.VMEM((a, rows, depth), BF16),
            pltpu.VMEM((a, rows, depth), BF16),
            pltpu.VMEM((a, rows, depth), BF16),
            pltpu.VMEM((a, rows, depth), BF16),
            pltpu.SemaphoreType.DMA((3 * a + ranks - 1,)),
            pltpu.SemaphoreType.DMA((3 * a + ranks - 1,)),
        ],
        compiler_params=pltpu.CompilerParams(
            collective_id=1, has_side_effects=True, vmem_limit_bytes=VMEM_LIMIT
        ),
        name="finish",
    )(iq, weights, keys, block_pos, peers_i, own_i, own_t, peers_t, carried)
    return grad, own + jnp.sum(peers.astype(F32), axis=0)


def swap(value, ranks):
    return jnp.stack(
        [
            lax.ppermute(value, "head", [(i, (i + d) % ranks) for i in range(ranks)])
            for d in range(1, ranks)
        ]
    )


def body(queries, latents, index_queries, index_keys, head_weights, block_pos):
    rows, heads, rank = queries.shape
    depth = index_queries.shape[2]
    n, ranks = lax.axis_size("ctx"), lax.axis_size("head")
    seq = rows * n
    q = jnp.transpose(queries, (1, 2, 0))
    iq = index_queries.reshape(rows * heads, depth)
    weights = jnp.transpose(head_weights)

    lat, keys, *own_i = gather(jnp.transpose(latents), index_keys, iq, weights, heads, n)
    lat = lat.reshape(seq, rank)
    keys = keys.reshape(seq, depth)
    peers_i = [swap(value, ranks) for value in own_i]
    own_t, peers_t = [], []
    for k in range(2):
        full, low = attend(q, lat, block_pos, k, n)
        own_t.append(full)
        peers_t.append(swap(low, ranks))
    first, carried = back(
        iq, weights, keys, block_pos, peers_i[0], own_i[0], own_t[0], peers_t[0], heads
    )
    second, grad_keys = finish(
        iq, weights, keys, block_pos, peers_i[1], own_i[1], own_t[1], peers_t[1], carried, heads,
        n, ranks,
    )
    grad = lax.dynamic_update_slice(first, second, (second.shape[0], 0))
    return grad.reshape(rows, heads, depth), grad_keys


def solution(mesh):
    return jax.shard_map(
        body,
        mesh=mesh,
        in_specs=(
            P("ctx", "head", None),
            P("ctx", None),
            P("ctx", "head", None),
            P("ctx", None),
            P("ctx", "head"),
            P(),
        ),
        out_specs=(P("ctx", "head", None), P("ctx", None)),
        check_vma=False,
    )
```
